512 devices in a mesh: req: 64 (over y, z), tp: 8 (over x, core).
Axes of the slice: x: 4, y: 8, z: 8, core: 2. Of those that a mesh axis runs over, the one named last changes fastest.
Arguments:
- queries: bfloat16 [1024, 4096], P('req', 'tp')
- kv_cache: bfloat16 [1024, 2, 128, 1024], P('req', None, None, 'tp')
- page_table: int32 [256, 4], P('req'), may hold values from 0 to 15, as said below
- cache_lengths: int32 [256], P('req'), may hold values from 1 to 512, as said below
- residual: bfloat16 [1024, 4096], P('req'), may hold values from -6 to 6
- out_weight: bfloat16 [4096, 4096], P('req', 'tp'), may hold values from -0.09375 to 0.09375
- norm_gain: float32 [4096], replicated, may hold values from 0.5 to 1.5
- router: bfloat16 [4096, 8], replicated, may hold values from -0.09375 to 0.09375
- gate_weight: bfloat16 [8, 4096, 8192], P('tp', None, 'req'), may hold values from -0.09375 to 0.09375
- up_weight: bfloat16 [8, 4096, 8192], P('tp', None, 'req'), may hold values from -0.09375 to 0.09375
- down_weight: bfloat16 [8, 4096, 8192], P('tp', 'req'), may hold values from -0.0625 to 0.0625
- expert_ids: int32 [1024, 2], P('req'), may hold values from 0 to 7, all different within a row; in each aligned block of 16 rows (0 to 15, 16 to 31, ...) at most 8 rows name the same one
Outputs:
- layer_out: bfloat16 [1024, 4096], P('req')
The draws below stay inside these ranges and needn't reach their ends.
Inputs may be any that keep to these rules, and one draw needn't show every extreme that they name: `page_table`: the 4 rows of one group together name each of that group's 16 pages once. `cache_lengths`: the first request of each group holds at least 13 positions. `expert_ids`: among the rows of one group no expert is named by more than 8 rows, a bound that some block reaches.
All inputs are finite; a program needn't handle non-finite values.
Results may differ from the reference program's by a relative error of at most 0.006.
Values may be sent and summed in bfloat16 or wider, within the bound.
A program may use at most 64 MiB of HBM per device.

```python
import math
import jax
import jax.numpy as jnp
import numpy as np
from jax import lax

D = 4096
HQ = 32
KVH = 8
HD = 128
EXPERTS = 8
FF = 8192
PAGE = 128
MAX_PAGES = 4
SEQ_DEV = 4
TOK_DEV = 16
PF_ROWS = 13
CAP = 8
CTX = 512
PAGES_DEV = 16
TOKENS = 1024
REQUESTS = 256
PAGES = 1024
N_REQ = 64


def draw_queries(key, part):
    base = jax.random.normal(jax.random.fold_in(key, 1), (TOKENS, HQ, HD), jnp.float32)
    return base.reshape(TOKENS, HQ * HD).astype(jnp.bfloat16)


def draw_kv_cache(key, part):
    keys = jax.random.normal(jax.random.fold_in(key, 3), (PAGES, PAGE, KVH, HD), jnp.float32)
    values = jax.random.normal(jax.random.fold_in(key, 4), (PAGES, PAGE, KVH, HD), jnp.float32)
    stacked = jnp.stack([keys, values], axis=1)
    return stacked.reshape(PAGES, 2, PAGE, KVH * HD).astype(jnp.bfloat16)


def draw_page_table(key, part):
    groups = PAGES // PAGES_DEV
    group_keys = jax.random.split(jax.random.fold_in(key, 6), groups)
    perms = jax.vmap(lambda single: jax.random.permutation(single, PAGES_DEV))(group_keys)
    return perms.reshape(REQUESTS, MAX_PAGES).astype(jnp.int32)


def draw_cache_lengths(key, part):
    position = jnp.arange(REQUESTS, dtype=jnp.int32)
    lowest = jnp.where(position % SEQ_DEV == 0, PF_ROWS, 1)
    drawn = jax.random.randint(jax.random.fold_in(key, 7), (REQUESTS,), 0, 1 << 20, dtype=jnp.int32)
    lengths = lowest + drawn % (CTX + 1 - lowest)
    picked = jax.random.randint(jax.random.fold_in(key, 8), (), 0, REQUESTS, dtype=jnp.int32)
    return jnp.where(position == picked, CTX, lengths).astype(jnp.int32)


def steps_of(key, shape, cuts, low, top_value):
    def one(dim, shards_of):
        draws = jax.random.uniform(jax.random.fold_in(jax.random.fold_in(key, 6), dim), (shards_of,), jnp.float32, low / len(cuts), top_value / len(cuts))
        return jnp.repeat(jnp.exp(draws), shape[dim] // shards_of).reshape((-1,) + (1,) * (len(shape) - dim - 1))

    level = one(*cuts[0])
    for cut in cuts[1:]:
        level = level * one(*cut)
    return level


def deal_out(rng, own, number, rows, number_of, top, limit, slope):
    order = jax.random.permutation(rng, number_of)
    packed, common = portions_of(number_of, rows * top, limit, slope, True), portions_of(number_of, rows * top, limit, slope, False)
    places = jnp.arange(number_of)

    def named(tallies, offset_by):
        used = int((tallies > 0).sum())
        fixed = max(1, used // 4)
        passed = fixed + (places - fixed + offset_by * (used - fixed)) % max(1, number_of - fixed)
        return jnp.zeros((number_of,), jnp.int32).at[order[jnp.where(places < fixed, places, passed)]].set(jnp.asarray(tallies, jnp.int32))

    tallies = jnp.where(number % 4 == 0, named(packed, number // 4), named(common, number - number // 4 - 1))
    mixed = jax.random.permutation(jax.random.fold_in(own, 3), number_of)
    source_of, taker = mixed[0:number_of // 2 * 2:2], mixed[1:number_of // 2 * 2:2]
    slack = jnp.minimum(tallies[source_of] - 1, limit - tallies[taker]) // 2
    slack = jnp.where((source_of == order[0]) | (taker == order[0]) | (tallies[taker] == 0), 0, jnp.maximum(slack, 0))
    passed = jax.random.randint(jax.random.fold_in(own, 4), (number_of // 2,), 0, 1 << 20) % (slack + 1)
    tallies = tallies.at[source_of].add(-passed).at[taker].add(passed)
    labels = jnp.searchsorted(jnp.cumsum(tallies), jnp.arange(rows * top), side="right").astype(jnp.int32)
    table = labels.reshape(top, rows).T
    table = table[jax.random.permutation(jax.random.fold_in(own, 1), rows)]
    offset_by = jax.random.randint(jax.random.fold_in(own, 2), (rows, 1), 0, top)
    return jnp.take_along_axis(table, (jnp.arange(top)[None, :] + offset_by) % top, axis=1)


def portions_of(number_of, total, limit, skew, full):
    loads = [(1 << 20) // math.isqrt(standing ** skew) + 1 for standing in range(1, number_of + 1)]
    largest = limit if full else min(limit, max(-(-total // number_of), total * loads[0] // sum(loads)))
    least = 1 if total - largest >= number_of - 1 else 0
    holding, rest = [largest] + [least] * (number_of - 1), total - largest - least * (number_of - 1)
    while rest > 0:
        movable = [i for i in range(1, number_of) if holding[i] < largest] or [i for i in range(1, number_of) if holding[i] < limit]
        mass, remaining = sum([loads[i] for i in movable]), rest
        for i in movable:
            extra = min(limit - holding[i], max(1, remaining * loads[i] // mass), rest)
            holding[i] = holding[i] + extra
            rest = rest - extra
    return np.array(holding)


def bell_draw(key, extent, scale, most, cuts=(), held_as=jnp.bfloat16):
    values = scale * jax.random.normal(key, extent, jnp.float32)
    if cuts:
        values = values * steps_of(key, extent, cuts, -0.22, 0.18)
    return jnp.clip(values, -most, most).astype(held_as)


def setup_inputs(seed: int = 0) -> dict:
    streams_of = jax.random.split(jax.random.key(seed), 13)
    queries = draw_queries(jax.random.fold_in(streams_of[12], 71), 0)
    kv_cache = draw_kv_cache(jax.random.fold_in(streams_of[12], 71), 0)
    page_table = draw_page_table(jax.random.fold_in(streams_of[12], 71), 0)
    cache_lengths = draw_cache_lengths(jax.random.fold_in(streams_of[12], 71), 0)
    residual = bell_draw(streams_of[4], (TOKENS, D), 1.0, 6.0, ((0, 64),))
    out_weight = bell_draw(streams_of[5], (D, HQ * HD), (HQ * HD) ** -0.5, 0.09375, ((0, 64), (1, 8)))
    norm_gain = jnp.clip(jax.random.uniform(streams_of[6], (D,), jnp.float32, 0.5, 1.5), 0.5, 1.5)
    router = bell_draw(streams_of[7], (D, EXPERTS), D ** -0.5, 0.09375)
    gate_weight = bell_draw(streams_of[8], (EXPERTS, D, FF), D ** -0.5, 0.09375, ((0, 8), (2, 64)))
    up_weight = bell_draw(streams_of[9], (EXPERTS, D, FF), D ** -0.5, 0.09375, ((0, 8), (2, 64)))
    down_weight = bell_draw(streams_of[10], (EXPERTS, D, FF), FF ** -0.5, 0.0625, ((0, 8), (1, 64)))
    expert_ids_keys = jax.random.split(jax.random.fold_in(streams_of[11], 1), TOKENS // TOK_DEV)
    expert_ids_turns = jax.random.permutation(jax.random.fold_in(streams_of[11], 3), TOKENS // TOK_DEV)
    expert_ids = jax.vmap(lambda own, number: deal_out(jax.random.fold_in(streams_of[11], 2), own, number, TOK_DEV, EXPERTS, 2, CAP, 2))(expert_ids_keys, expert_ids_turns).reshape((TOKENS, 2))
    return dict(queries=queries, kv_cache=kv_cache, page_table=page_table, cache_lengths=cache_lengths, residual=residual, out_weight=out_weight, norm_gain=norm_gain, router=router, gate_weight=gate_weight, up_weight=up_weight, down_weight=down_weight, expert_ids=expert_ids)


def attend(queries, pool, table, lengths):
    row_count = queries.shape[0]
    slot_count = lengths.shape[0]
    page_size = pool.shape[2]
    kv_width = pool.shape[3] // HD
    group_size = queries.shape[1] // pool.shape[3]
    context = table.shape[1] * page_size
    prefill = row_count - slot_count + 1
    row_index = jnp.arange(row_count, dtype=jnp.int32)
    row_slot = jnp.maximum(row_index - prefill + 1, 0)
    slot_match = row_slot[:, None] == jnp.arange(slot_count, dtype=jnp.int32)[None, :]
    row_length = lax.optimization_barrier(jnp.sum(jnp.where(slot_match, lengths[None, :], 0), axis=1))
    row_position = jnp.where(row_index < prefill, row_length - prefill + row_index, row_length - 1)
    pages = jnp.take(pool, table.reshape(-1).astype(jnp.int32), axis=0)
    keys = pages[:, 0].reshape(slot_count * context, kv_width, HD)
    values = pages[:, 1].reshape(slot_count * context, kv_width, HD)
    key_index = jnp.arange(slot_count * context, dtype=jnp.int32)
    valid = ((key_index // context)[None, :] == row_slot[:, None]) & ((key_index % context)[None, :] <= row_position[:, None])
    shaped = queries.reshape(row_count, kv_width, group_size, HD)
    scores = jnp.einsum('rkgd,skd->rkgs', shaped.astype(jnp.float32), keys.astype(jnp.float32)) * (1.0 / HD ** 0.5)
    usable = valid[:, None, None, :]
    masked = jnp.where(usable, scores, -1e+30)
    peak = lax.optimization_barrier(jnp.max(masked, axis=3, keepdims=True))
    weights = jnp.where(usable, jnp.exp(masked - peak), 0.0)
    probs = (weights / lax.optimization_barrier(jnp.sum(weights, axis=3, keepdims=True))).astype(jnp.bfloat16)
    mixed = jnp.einsum('rkgs,skd->rkgd', probs.astype(jnp.float32), values.astype(jnp.float32))
    return mixed.reshape(row_count, kv_width * group_size * HD).astype(jnp.bfloat16)

def reference(queries, kv_cache, page_table, cache_lengths, residual, out_weight, norm_gain, router, gate_weight, up_weight, down_weight, expert_ids):
    grouped = (queries.reshape(N_REQ, TOK_DEV, HQ * HD), kv_cache.reshape(N_REQ, PAGES_DEV, 2, PAGE, KVH * HD), page_table.reshape(N_REQ, SEQ_DEV, MAX_PAGES), cache_lengths.reshape(N_REQ, SEQ_DEV))
    attended = lax.map(lambda group: attend(*group), grouped).reshape(TOKENS, HQ * HD)
    projected = lax.dot_general(attended, out_weight, (((1,), (1,)), ((), ())), preferred_element_type=jnp.float32)
    hidden_state = residual.astype(jnp.float32) + projected
    inverse = lax.rsqrt(lax.optimization_barrier(jnp.mean(hidden_state * hidden_state, axis=1, keepdims=True)) + 1e-05)
    normed = (hidden_state * inverse * norm_gain[None, :]).astype(jnp.bfloat16)
    logits = jnp.dot(normed, router, preferred_element_type=jnp.float32)
    expert_range = jnp.arange(EXPERTS, dtype=jnp.int32)
    chosen = lax.optimization_barrier(jnp.sum(jnp.where(expert_ids[:, :, None] == expert_range[None, None, :], logits[:, None, :], 0.0), axis=2))
    first = jax.nn.sigmoid(chosen[:, 0] - chosen[:, 1])
    mixing = jnp.stack([first, 1.0 - first], axis=1)
    flat = expert_ids.reshape(N_REQ, 2 * TOK_DEV)
    onehot = (flat[:, :, None] == expert_range[None, None, :]).astype(jnp.int32)
    before = jnp.cumsum(onehot, axis=1) - onehot
    slot = lax.optimization_barrier(jnp.sum(before * onehot, axis=2))
    capacity_range = jnp.arange(CAP, dtype=jnp.int32)
    select = (flat[:, None, None, :] == expert_range[None, :, None, None]) & (slot[:, None, None, :] == capacity_range[None, None, :, None])
    repeated = jnp.repeat(normed.reshape(N_REQ, TOK_DEV, D), 2, axis=1)
    dispatched = jnp.einsum('gecr,grd->gecd', select.astype(jnp.float32), repeated.astype(jnp.float32)).astype(jnp.bfloat16)

    def run_expert(operands):
        block, gate_part, up_part, down_part = operands
        flat_rows = block.reshape(N_REQ * CAP, D)
        gate = jnp.dot(flat_rows, gate_part, preferred_element_type=jnp.float32)
        upward = jnp.dot(flat_rows, up_part, preferred_element_type=jnp.float32)
        activated = (jax.nn.silu(gate) * upward).astype(jnp.bfloat16)
        result = lax.dot_general(activated, down_part, (((1,), (1,)), ((), ())), preferred_element_type=jnp.float32)
        return result.astype(jnp.bfloat16).reshape(N_REQ, CAP, D)
    outputs = lax.map(run_expert, (jnp.moveaxis(dispatched, 1, 0), gate_weight, up_weight, down_weight))
    gathered = jnp.einsum('gecr,egcd->grd', select.astype(jnp.float32), outputs.astype(jnp.float32))
    weighted = gathered * mixing.reshape(N_REQ, 2 * TOK_DEV)[:, :, None]
    expert_mix = lax.optimization_barrier(jnp.sum(weighted.reshape(TOKENS, 2, D), axis=1))
    return (hidden_state + expert_mix).astype(jnp.bfloat16)
```

```python
import functools

import jax
import jax.numpy as jnp
from jax import lax
from jax.experimental import pallas as pl
from jax.experimental.pallas import tpu as pltpu
from jax.sharding import PartitionSpec as P

D = 4096
HD = 128
EXPERTS = 8
CAP = 8
TP = 8

MESH = pl.DeviceIdType.MESH
NY = 8
NZ = 8


def gather_kernel(split, x_ref, out_ref, own_sem, send_sem, recv_sem):
    me = lax.axis_index("req")
    sign = 1 - 2 * (lax.axis_index("tp") % 2)
    y, z = me // NZ, me % NZ

    def at_z(step):
        return (z + sign * step + 2 * NZ) % NZ

    def at_y(step):
        return (y + sign * step + 2 * NY) % NY

    neighbours = [
        {"req": y * NZ + at_z(1)},
        {"req": y * NZ + at_z(-1)},
        {"req": at_y(1) * NZ + z},
        {"req": at_y(-1) * NZ + z},
    ]
    barrier = pltpu.get_barrier_semaphore()
    for neighbour in neighbours:
        pl.semaphore_signal(barrier, inc=1, device_id=neighbour, device_id_type=MESH)
    pl.semaphore_wait(barrier, 4)
    own = pltpu.make_async_copy(x_ref, out_ref.at[y, z], own_sem)
    own.start()
    rows, columns = x_ref.shape
    if split == 0:
        halves = [
            (pl.ds(0, rows // 2), slice(None)),
            (pl.ds(rows // 2, rows // 2), slice(None)),
        ]
    else:
        halves = [
            (slice(None), pl.ds(0, columns // 2)),
            (slice(None), pl.ds(columns // 2, columns // 2)),
        ]

    def place(phase, stream, step):
        way = 1 if stream % 2 == 0 else -1
        half = halves[stream // 2]
        if phase == 0:
            if stream < 2:
                return out_ref.at[(y, at_z(-way * step)) + half]
            return out_ref.at[(at_y(-way * step), z) + half]
        if stream < 2:
            return out_ref.at[(at_y(-way * step), slice(None)) + half]
        return out_ref.at[(slice(None), at_z(-way * step)) + half]

    def target(phase, stream):
        return neighbours[stream] if phase == 0 else neighbours[(stream + 2) % 4]

    everything = []
    for phase in range(2):
        copies = {}
        for step in range(4):
            for stream in range(4):
                if stream % 2 == 1 and step == 3:
                    continue
                if step > 0:
                    copies[stream, step - 1].wait_recv()
                source = place(phase, stream, step)
                if phase == 0 and step == 0:
                    source = x_ref.at[halves[stream // 2]]
                copy = pltpu.make_async_remote_copy(
                    src_ref=source,
                    dst_ref=place(phase, stream, step),
                    send_sem=send_sem.at[phase, stream, step],
                    recv_sem=recv_sem.at[phase, stream, step],
                    device_id=target(phase, stream),
                    device_id_type=MESH,
                )
                copy.start()
                copies[stream, step] = copy
                everything.append(copy)
        for stream in range(4):
            copies[stream, 2 if stream % 2 else 3].wait_recv()
        if phase == 0:
            own.wait()
    for copy in everything:
        copy.wait_send()


def gather(chunk, split, number):
    rows, columns = chunk.shape
    return pl.pallas_call(
        functools.partial(gather_kernel, split),
        out_shape=jax.ShapeDtypeStruct((NY, NZ, rows, columns), chunk.dtype),
        in_specs=[pl.BlockSpec(memory_space=pltpu.VMEM)],
        out_specs=pl.BlockSpec(memory_space=pl.ANY),
        scratch_shapes=[
            pltpu.SemaphoreType.DMA(()),
            pltpu.SemaphoreType.DMA((2, 4, 4)),
            pltpu.SemaphoreType.DMA((2, 4, 4)),
        ],
        compiler_params=pltpu.CompilerParams(collective_id=number, has_side_effects=True),
    )(chunk)


def total_kernel(n, x_ref, out_ref, parts, own, own_sem, send_sem, recv_sem):
    me = lax.axis_index("tp")
    width = x_ref.shape[1] // n
    barrier = pltpu.get_barrier_semaphore()
    for step in range(1, n):
        pl.semaphore_signal(
            barrier, inc=1, device_id={"tp": (me + step) % n}, device_id_type=MESH
        )
    pl.semaphore_wait(barrier, n - 1)

    def columns(index):
        return pl.ds(pl.multiple_of(index * width, width), width)

    scatter = []
    for step in range(1, n):
        peer = (me + step) % n
        copy = pltpu.make_async_remote_copy(
            src_ref=x_ref.at[:, columns(peer)],
            dst_ref=parts.at[step - 1],
            send_sem=send_sem.at[0, step - 1],
            recv_sem=recv_sem.at[0, step - 1],
            device_id={"tp": peer},
            device_id_type=MESH,
        )
        copy.start()
        scatter.append(copy)
    total = x_ref[:, columns(me)].astype(jnp.float32)
    for step in range(1, n):
        scatter[step - 1].wait_recv()
        total = total + parts[step - 1].astype(jnp.float32)
    own[...] = total.astype(own.dtype)
    spread = []
    for step in range(1, n):
        peer = (me + step) % n
        copy = pltpu.make_async_remote_copy(
            src_ref=own,
            dst_ref=out_ref.at[:, columns(me)],
            send_sem=send_sem.at[1, step - 1],
            recv_sem=recv_sem.at[1, step - 1],
            device_id={"tp": peer},
            device_id_type=MESH,
        )
        copy.start()
        spread.append(copy)
    mine = pltpu.make_async_copy(own, out_ref.at[:, columns(me)], own_sem)
    mine.start()
    for copy in scatter:
        copy.wait_send()
    for copy in spread:
        copy.wait_recv()
    for copy in spread:
        copy.wait_send()
    mine.wait()


def total_over_tp(x, n, number):
    rows, columns = x.shape
    return pl.pallas_call(
        functools.partial(total_kernel, n),
        out_shape=jax.ShapeDtypeStruct(x.shape, x.dtype),
        in_specs=[pl.BlockSpec(memory_space=pltpu.VMEM)],
        out_specs=pl.BlockSpec(memory_space=pltpu.VMEM),
        scratch_shapes=[
            pltpu.VMEM((n - 1, rows, columns // n), x.dtype),
            pltpu.VMEM((rows, columns // n), x.dtype),
            pltpu.SemaphoreType.DMA(()),
            pltpu.SemaphoreType.DMA((2, n - 1)),
            pltpu.SemaphoreType.DMA((2, n - 1)),
        ],
        compiler_params=pltpu.CompilerParams(collective_id=number, has_side_effects=True),
    )(x)


def attend(queries, pool, table, lengths):
    row_count = queries.shape[0]
    slot_count = lengths.shape[0]
    page_size = pool.shape[2]
    kv_width = pool.shape[3] // HD
    group_size = queries.shape[1] // pool.shape[3]
    context = table.shape[1] * page_size
    prefill = row_count - slot_count + 1
    row_index = jnp.arange(row_count, dtype=jnp.int32)
    row_slot = jnp.maximum(row_index - prefill + 1, 0)
    slot_match = row_slot[:, None] == jnp.arange(slot_count, dtype=jnp.int32)[None, :]
    row_length = jnp.sum(jnp.where(slot_match, lengths[None, :], 0), axis=1)
    row_position = jnp.where(row_index < prefill, row_length - prefill + row_index, row_length - 1)
    pages = jnp.take(pool, table.reshape(-1), axis=0)
    keys = pages[:, 0].reshape(slot_count * context, kv_width, HD)
    values = pages[:, 1].reshape(slot_count * context, kv_width, HD)
    key_index = jnp.arange(slot_count * context, dtype=jnp.int32)
    valid = ((key_index // context)[None, :] == row_slot[:, None]) & (
        (key_index % context)[None, :] <= row_position[:, None]
    )
    shaped = queries.reshape(row_count, kv_width, group_size, HD)
    scores = jnp.einsum("rkgd,skd->rkgs", shaped, keys, preferred_element_type=jnp.float32) * (
        1.0 / HD**0.5
    )
    usable = valid[:, None, None, :]
    masked = jnp.where(usable, scores, -1e30)
    peak = jnp.max(masked, axis=3, keepdims=True)
    weights = jnp.where(usable, jnp.exp(masked - peak), 0.0)
    probs = (weights / jnp.sum(weights, axis=3, keepdims=True)).astype(jnp.bfloat16)
    mixed = jnp.einsum("rkgs,skd->rkgd", probs, values, preferred_element_type=jnp.float32)
    return mixed.reshape(row_count, kv_width * group_size * HD).astype(jnp.bfloat16)


def per_device(
    queries,
    kv_cache,
    page_table,
    cache_lengths,
    residual,
    out_weight,
    norm_gain,
    router,
    gate_weight,
    up_weight,
    down_weight,
    expert_ids,
):
    attended = attend(queries, kv_cache, page_table, cache_lengths)
    contract_last = (((1,), (1,)), ((), ()))
    partial_value = lax.dot_general(
        attended,
        gather(out_weight, 1, 1).reshape(D, out_weight.shape[1]),
        contract_last,
        preferred_element_type=jnp.float32,
    )
    projected = total_over_tp(partial_value, TP, 2)
    hidden_state = residual.astype(jnp.float32) + projected
    inverse = lax.rsqrt(jnp.mean(hidden_state * hidden_state, axis=1, keepdims=True) + 1e-05)
    normed = (hidden_state * inverse * norm_gain[None, :]).astype(jnp.bfloat16)
    logits = jnp.dot(normed, router, preferred_element_type=jnp.float32)
    expert_range = jnp.arange(EXPERTS, dtype=jnp.int32)
    chosen = jnp.sum(
        jnp.where(expert_ids[:, :, None] == expert_range[None, None, :], logits[:, None, :], 0.0),
        axis=2,
    )
    first = jax.nn.sigmoid(chosen[:, 0] - chosen[:, 1])
    mixing = jnp.stack([first, 1.0 - first], axis=1).reshape(-1)
    flat = expert_ids.reshape(-1)
    onehot = (flat[:, None] == expert_range[None, :]).astype(jnp.int32)
    before = jnp.cumsum(onehot, axis=0) - onehot
    slot = jnp.sum(before * onehot, axis=1)
    local_experts = gate_weight.shape[0]
    owned = lax.axis_index("tp") * local_experts + jnp.arange(local_experts, dtype=jnp.int32)
    capacity_range = jnp.arange(CAP, dtype=jnp.int32)
    select = (flat[None, None, :] == owned[:, None, None]) & (
        slot[None, None, :] == capacity_range[None, :, None]
    )
    repeated = jnp.repeat(normed, 2, axis=0)
    dispatched = jnp.einsum(
        "ecr,rd->ecd", select.astype(jnp.bfloat16), repeated, preferred_element_type=jnp.float32
    ).astype(jnp.bfloat16)[0]
    shard_piece = gather(dispatched, 1, 3).reshape(-1, D)
    gate = jnp.dot(shard_piece, gate_weight[0], preferred_element_type=jnp.float32)
    upward = jnp.dot(shard_piece, up_weight[0], preferred_element_type=jnp.float32)
    activated = (jax.nn.silu(gate) * upward).astype(jnp.bfloat16)
    units = gather(activated, 0, 4).reshape(-1, *activated.shape)
    columns = jnp.einsum(
        "rsf,drf->sd",
        units,
        down_weight[0].reshape(down_weight.shape[1], units.shape[0], units.shape[2]),
        preferred_element_type=jnp.float32,
    ).reshape(units.shape[0], 1, CAP, -1)
    returned = lax.all_to_all(
        columns.astype(jnp.bfloat16), "req", split_axis=0, concat_axis=3, tiled=True
    )
    outputs = returned.reshape(local_experts, CAP, D)
    gathered = jnp.einsum("ecr,ecd->rd", select.astype(jnp.float32), outputs.astype(jnp.float32))
    weighted = gathered * mixing[:, None]
    local_mix = jnp.sum(weighted.reshape(residual.shape[0], 2, D), axis=1)
    expert_mix = total_over_tp(local_mix.astype(jnp.bfloat16), TP, 5).astype(jnp.float32)
    return (hidden_state + expert_mix).astype(jnp.bfloat16)


def solution(mesh):
    return jax.shard_map(
        per_device,
        mesh=mesh,
        in_specs=(
            P("req", "tp"),
            P("req", None, None, "tp"),
            P("req", None),
            P("req"),
            P("req", None),
            P("req", "tp"),
            P(),
            P(),
            P("tp", None, "req"),
            P("tp", None, "req"),
            P("tp", "req", None),
            P("req", None),
        ),
        out_specs=P("req", None),
        check_vma=False,
    )
```

```python
import functools

import jax
import jax.numpy as jnp
from jax import lax
from jax.experimental import pallas as pl
from jax.experimental.pallas import tpu as pltpu
from jax.sharding import PartitionSpec as P

D = 4096
HD = 128
EXPERTS = 8
CAP = 8
TP = 8

MESH = pl.DeviceIdType.MESH
NY = 8
NZ = 8


def place_of(me, swap):
    y, z = me // NZ, me % NZ
    return z + swap * (y - z), y + swap * (z - y)


def index_of(a, b, swap):
    return (b + swap * (a - b)) * NZ + a + swap * (b - a)


def gather_kernel(split, with_down, *refs):
    if with_down:
        x_ref, down_ref, out_ref, laid_ref, own_sem, send_sem, recv_sem, lay_send, lay_recv = refs
    else:
        x_ref, out_ref, own_sem, send_sem, recv_sem = refs
    me = lax.axis_index("req")
    swap = lax.axis_index("tp") % 2
    sign = 1 - 2 * swap
    y, z = me // NZ, me % NZ

    def at_z(step):
        return (z + sign * step + 2 * NZ) % NZ

    def at_y(step):
        return (y + sign * step + 2 * NY) % NY

    neighbours = [
        {1: y * NZ + at_z(1), -1: y * NZ + at_z(-1)},
        {1: at_y(1) * NZ + z, -1: at_y(-1) * NZ + z},
    ]
    a, b = place_of(me, swap)
    barrier = pltpu.get_barrier_semaphore()
    if with_down:
        for step in range(NY):
            for other in (y * NZ + (z + step) % NZ, ((y + step) % NY) * NZ + z):
                if step:
                    pl.semaphore_signal(
                        barrier, inc=1, device_id={"req": other}, device_id_type=MESH
                    )
        pl.semaphore_wait(barrier, 2 * (NY - 1))
    else:
        for axis in range(2):
            for way in (1, -1):
                pl.semaphore_signal(
                    barrier,
                    inc=1,
                    device_id={"req": neighbours[axis][way]},
                    device_id_type=MESH,
                )
        pl.semaphore_wait(barrier, 4)
    own = pltpu.make_async_copy(x_ref, out_ref.at[y, z], own_sem)
    own.start()
    rows, columns = x_ref.shape
    if split == 0:
        halves = [
            (pl.ds(0, rows // 2), slice(None)),
            (pl.ds(rows // 2, rows // 2), slice(None)),
        ]
    else:
        halves = [
            (slice(None), pl.ds(0, columns // 2)),
            (slice(None), pl.ds(columns // 2, columns // 2)),
        ]

    plan = []
    for half in range(2):
        for way, steps in ((1, 4), (-1, 3)):
            for step in range(steps):
                needs = (half, 1, way, 0, step - 1) if step else None
                plan.append((step, 0, (half, 1, way, 0, step), needs))
                for far in (0, -1, 1, -2, 2, -3, 3, -4):
                    if step:
                        needs = (half, 2, way, far, step - 1)
                    elif far:
                        needs = (half, 1, 1 if far < 0 else -1, 0, abs(far) - 1)
                    else:
                        needs = None
                    plan.append((abs(far) + step, 1, (half, 2, way, far, step), needs))
    plan.sort(key=lambda entry: entry[:2])
    copies, landed, laid = {}, set(), []
    level = -1
    for entry, (stage, _, key, needs) in enumerate(plan):
        if with_down and stage > level:
            level = stage
            for step in range(1, NY):
                to = (b + step) % NY
                width = pl.ds(pl.multiple_of(index_of(level, to, swap) * 128, 128), 128)
                copy = pltpu.make_async_remote_copy(
                    src_ref=down_ref.at[:, width],
                    dst_ref=laid_ref.at[b, :, pl.ds(level * 128, 128)],
                    send_sem=lay_send.at[step - 1, level],
                    recv_sem=lay_recv.at[step - 1, level],
                    device_id={"req": index_of(a, to, swap)},
                    device_id_type=MESH,
                )
                copy.start()
                laid.append(copy)
        half, phase, way, far, step = key
        if needs is not None and needs not in landed:
            copies[needs].wait_recv()
            landed.add(needs)
        one, two = (-way * step, 0) if phase == 1 else (far, -way * step)
        where = (at_y(two), at_z(one)) if half == 0 else (at_y(one), at_z(two))
        region = out_ref.at[where + halves[half]]
        first = step == 0 and far == 0
        copy = pltpu.make_async_remote_copy(
            src_ref=x_ref.at[halves[half]] if first else region,
            dst_ref=region,
            send_sem=send_sem.at[entry],
            recv_sem=recv_sem.at[entry],
            device_id={"req": neighbours[(half + phase - 1) % 2][way]},
            device_id_type=MESH,
        )
        copy.start()
        copies[key] = copy
    if with_down:
        for far in range(NY):
            width = pl.ds(pl.multiple_of(index_of(far, b, swap) * 128, 128), 128)
            laid_ref[b, :, pl.ds(far * 128, 128)] = down_ref[:, width]
    for key, copy in copies.items():
        if key not in landed:
            copy.wait_recv()
    own.wait()
    for copy in copies.values():
        copy.wait_send()
    for copy in laid:
        copy.wait_recv()
    for copy in laid:
        copy.wait_send()


def gather(chunk, split, number, down=None):
    rows, columns = chunk.shape
    shapes = [jax.ShapeDtypeStruct((NY, NZ, rows, columns), chunk.dtype)]
    out_specs = [pl.BlockSpec(memory_space=pl.ANY)]
    scratch = [
        pltpu.SemaphoreType.DMA(()),
        pltpu.SemaphoreType.DMA((126,)),
        pltpu.SemaphoreType.DMA((126,)),
    ]
    operands = [chunk]
    if down is not None:
        operands.append(down)
        shapes.append(
            jax.ShapeDtypeStruct((NY, down.shape[0], down.shape[1] // NY), down.dtype)
        )
        out_specs.append(pl.BlockSpec(memory_space=pltpu.VMEM))
        scratch += [pltpu.SemaphoreType.DMA((7, 8)), pltpu.SemaphoreType.DMA((7, 8))]
    result = pl.pallas_call(
        functools.partial(gather_kernel, split, down is not None),
        out_shape=shapes,
        in_specs=[pl.BlockSpec(memory_space=pltpu.VMEM)] * len(operands),
        out_specs=out_specs,
        scratch_shapes=scratch,
        compiler_params=pltpu.CompilerParams(collective_id=number, has_side_effects=True),
    )(*operands)
    return result if down is not None else result[0]


def down_kernel(x_ref, laid_ref, out_ref, units, partial, landing, ring_send, ring_recv, send_sem, recv_sem):
    me = lax.axis_index("req")
    swap = lax.axis_index("tp") % 2
    a, b = place_of(me, swap)
    groups = NY * NZ
    barrier = pltpu.get_barrier_semaphore()

    @pl.loop(1, groups)
    def _(step):
        pl.semaphore_signal(
            barrier,
            inc=1,
            device_id={"req": (me + step) % groups},
            device_id_type=MESH,
        )

    pl.semaphore_wait(barrier, groups - 1)

    def block(step):
        return pl.ds(pl.multiple_of(((a + step + NZ) % NZ) * 128, 128), 128)

    copies = {}
    for step in range(4):
        for way in (1, -1):
            if way == -1 and step == 3:
                continue
            if step:
                copies[way, step - 1].wait_recv()
            region = units.at[:, block(-way * step)]
            copy = pltpu.make_async_remote_copy(
                src_ref=region if step else x_ref,
                dst_ref=region,
                send_sem=ring_send.at[(1 - way) // 2, step],
                recv_sem=ring_recv.at[(1 - way) // 2, step],
                device_id={"req": index_of((a + way + NZ) % NZ, b, swap)},
                device_id_type=MESH,
            )
            copy.start()
            copies[way, step] = copy
        if step == 0:
            units[:, block(0)] = x_ref[...]
    copies[1, 3].wait_recv()
    copies[-1, 2].wait_recv()
    weights = laid_ref[...].reshape(laid_ref.shape[0] * laid_ref.shape[1], laid_ref.shape[2])
    product = lax.dot_general(
        units[...], weights, (((1,), (1,)), ((), ())), preferred_element_type=jnp.float32
    )
    partial[...] = product.astype(partial.dtype).reshape(partial.shape)

    def message(step):
        to = (me + step) % groups
        return pltpu.make_async_remote_copy(
            src_ref=partial.at[to],
            dst_ref=landing.at[b * NZ + a],
            send_sem=send_sem.at[step - 1],
            recv_sem=recv_sem.at[step - 1],
            device_id={"req": to},
            device_id_type=MESH,
        )

    @pl.loop(1, groups)
    def _(step):
        message(step).start()

    landing[b * NZ + a] = partial[me]

    @pl.loop(1, groups)
    def _(step):
        message(step).wait_recv()

    total = landing[pl.ds(0, NZ)].astype(jnp.float32)
    for row in range(1, NY):
        total = total + landing[pl.ds(row * NZ, NZ)].astype(jnp.float32)
    out_ref[...] = total

    @pl.loop(1, groups)
    def _(step):
        message(step).wait_send()

    for copy in copies.values():
        copy.wait_send()


def down_and_return(activated, laid, number):
    rows, width = activated.shape
    outs = laid.shape[0] * laid.shape[1]
    groups = NY * NZ
    return pl.pallas_call(
        down_kernel,
        out_shape=jax.ShapeDtypeStruct((NZ, rows // groups, outs), jnp.float32),
        in_specs=[pl.BlockSpec(memory_space=pltpu.VMEM)] * 2,
        out_specs=pl.BlockSpec(memory_space=pltpu.VMEM),
        scratch_shapes=[
            pltpu.VMEM((rows, NZ * width), activated.dtype),
            pltpu.VMEM((groups, rows // groups, outs), jnp.bfloat16),
            pltpu.VMEM((groups, rows // groups, outs), jnp.bfloat16),
            pltpu.SemaphoreType.DMA((2, 4)),
            pltpu.SemaphoreType.DMA((2, 4)),
            pltpu.SemaphoreType.DMA((groups - 1,)),
            pltpu.SemaphoreType.DMA((groups - 1,)),
        ],
        compiler_params=pltpu.CompilerParams(collective_id=number, has_side_effects=True),
    )(activated, laid)


def total_kernel(n, x_ref, out_ref, parts, own, own_sem, send_sem, recv_sem):
    me = lax.axis_index("tp")
    width = x_ref.shape[1] // n
    barrier = pltpu.get_barrier_semaphore()
    for step in range(1, n):
        pl.semaphore_signal(
            barrier, inc=1, device_id={"tp": (me + step) % n}, device_id_type=MESH
        )
    pl.semaphore_wait(barrier, n - 1)

    def columns(index):
        return pl.ds(pl.multiple_of(index * width, width), width)

    scatter = []
    for step in range(1, n):
        peer = (me + step) % n
        copy = pltpu.make_async_remote_copy(
            src_ref=x_ref.at[:, columns(peer)],
            dst_ref=parts.at[step - 1],
            send_sem=send_sem.at[0, step - 1],
            recv_sem=recv_sem.at[0, step - 1],
            device_id={"tp": peer},
            device_id_type=MESH,
        )
        copy.start()
        scatter.append(copy)
    total = x_ref[:, columns(me)].astype(jnp.float32)
    for step in range(1, n):
        scatter[step - 1].wait_recv()
        total = total + parts[step - 1].astype(jnp.float32)
    own[...] = total.astype(own.dtype)
    spread = []
    for step in range(1, n):
        peer = (me + step) % n
        copy = pltpu.make_async_remote_copy(
            src_ref=own,
            dst_ref=out_ref.at[:, columns(me)],
            send_sem=send_sem.at[1, step - 1],
            recv_sem=recv_sem.at[1, step - 1],
            device_id={"tp": peer},
            device_id_type=MESH,
        )
        copy.start()
        spread.append(copy)
    mine = pltpu.make_async_copy(own, out_ref.at[:, columns(me)], own_sem)
    mine.start()
    for copy in scatter:
        copy.wait_send()
    for copy in spread:
        copy.wait_recv()
    for copy in spread:
        copy.wait_send()
    mine.wait()


def total_over_tp(x, n, number):
    rows, columns = x.shape
    return pl.pallas_call(
        functools.partial(total_kernel, n),
        out_shape=jax.ShapeDtypeStruct(x.shape, x.dtype),
        in_specs=[pl.BlockSpec(memory_space=pltpu.VMEM)],
        out_specs=pl.BlockSpec(memory_space=pltpu.VMEM),
        scratch_shapes=[
            pltpu.VMEM((n - 1, rows, columns // n), x.dtype),
            pltpu.VMEM((rows, columns // n), x.dtype),
            pltpu.SemaphoreType.DMA(()),
            pltpu.SemaphoreType.DMA((2, n - 1)),
            pltpu.SemaphoreType.DMA((2, n - 1)),
        ],
        compiler_params=pltpu.CompilerParams(collective_id=number, has_side_effects=True),
    )(x)


def attend(queries, pool, table, lengths):
    row_count = queries.shape[0]
    slot_count = lengths.shape[0]
    page_size = pool.shape[2]
    kv_width = pool.shape[3] // HD
    group_size = queries.shape[1] // pool.shape[3]
    context = table.shape[1] * page_size
    prefill = row_count - slot_count + 1
    row_index = jnp.arange(row_count, dtype=jnp.int32)
    row_slot = jnp.maximum(row_index - prefill + 1, 0)
    slot_match = row_slot[:, None] == jnp.arange(slot_count, dtype=jnp.int32)[None, :]
    row_length = jnp.sum(jnp.where(slot_match, lengths[None, :], 0), axis=1)
    row_position = jnp.where(row_index < prefill, row_length - prefill + row_index, row_length - 1)
    pages = jnp.take(pool, table.reshape(-1), axis=0)
    keys = pages[:, 0].reshape(slot_count * context, kv_width, HD)
    values = pages[:, 1].reshape(slot_count * context, kv_width, HD)
    key_index = jnp.arange(slot_count * context, dtype=jnp.int32)
    valid = ((key_index // context)[None, :] == row_slot[:, None]) & (
        (key_index % context)[None, :] <= row_position[:, None]
    )
    shaped = queries.reshape(row_count, kv_width, group_size, HD)
    scores = jnp.einsum("rkgd,skd->rkgs", shaped, keys, preferred_element_type=jnp.float32) * (
        1.0 / HD**0.5
    )
    usable = valid[:, None, None, :]
    masked = jnp.where(usable, scores, -1e30)
    peak = jnp.max(masked, axis=3, keepdims=True)
    weights = jnp.where(usable, jnp.exp(masked - peak), 0.0)
    probs = (weights / jnp.sum(weights, axis=3, keepdims=True)).astype(jnp.bfloat16)
    mixed = jnp.einsum("rkgs,skd->rkgd", probs, values, preferred_element_type=jnp.float32)
    return mixed.reshape(row_count, kv_width * group_size * HD).astype(jnp.bfloat16)


def per_device(
    queries,
    kv_cache,
    page_table,
    cache_lengths,
    residual,
    out_weight,
    norm_gain,
    router,
    gate_weight,
    up_weight,
    down_weight,
    expert_ids,
):
    attended = attend(queries, kv_cache, page_table, cache_lengths)
    contract_last = (((1,), (1,)), ((), ()))
    all_weight, laid = gather(out_weight, 1, 1, down_weight[0])
    partial_value = lax.dot_general(
        attended,
        all_weight.reshape(D, out_weight.shape[1]),
        contract_last,
        preferred_element_type=jnp.float32,
    )
    projected = total_over_tp(partial_value, TP, 2)
    hidden_state = residual.astype(jnp.float32) + projected
    inverse = lax.rsqrt(jnp.mean(hidden_state * hidden_state, axis=1, keepdims=True) + 1e-05)
    normed = (hidden_state * inverse * norm_gain[None, :]).astype(jnp.bfloat16)
    logits = jnp.dot(normed, router, preferred_element_type=jnp.float32)
    expert_range = jnp.arange(EXPERTS, dtype=jnp.int32)
    chosen = jnp.sum(
        jnp.where(expert_ids[:, :, None] == expert_range[None, None, :], logits[:, None, :], 0.0),
        axis=2,
    )
    first = jax.nn.sigmoid(chosen[:, 0] - chosen[:, 1])
    mixing = jnp.stack([first, 1.0 - first], axis=1).reshape(-1)
    flat = expert_ids.reshape(-1)
    onehot = (flat[:, None] == expert_range[None, :]).astype(jnp.int32)
    before = jnp.cumsum(onehot, axis=0) - onehot
    slot = jnp.sum(before * onehot, axis=1)
    local_experts = gate_weight.shape[0]
    owned = lax.axis_index("tp") * local_experts + jnp.arange(local_experts, dtype=jnp.int32)
    capacity_range = jnp.arange(CAP, dtype=jnp.int32)
    select = (flat[None, None, :] == owned[:, None, None]) & (
        slot[None, None, :] == capacity_range[None, :, None]
    )
    repeated = jnp.repeat(normed, 2, axis=0)
    dispatched = jnp.einsum(
        "ecr,rd->ecd", select.astype(jnp.bfloat16), repeated, preferred_element_type=jnp.float32
    ).astype(jnp.bfloat16)[0]
    shard_piece = gather(dispatched, 1, 3).reshape(-1, D)
    gate = jnp.dot(shard_piece, gate_weight[0], preferred_element_type=jnp.float32)
    upward = jnp.dot(shard_piece, up_weight[0], preferred_element_type=jnp.float32)
    activated = (jax.nn.silu(gate) * upward).astype(jnp.bfloat16)
    pieces = down_and_return(activated, laid, 4).reshape(NZ, CAP, NY, -1)
    outputs = jnp.where(
        lax.axis_index("tp") % 2 == 0,
        jnp.transpose(pieces, (1, 2, 0, 3)),
        jnp.transpose(pieces, (1, 0, 2, 3)),
    ).reshape(local_experts, CAP, D)
    gathered = jnp.einsum("ecr,ecd->rd", select.astype(jnp.float32), outputs)
    weighted = gathered * mixing[:, None]
    local_mix = jnp.sum(weighted.reshape(residual.shape[0], 2, D), axis=1)
    expert_mix = total_over_tp(local_mix.astype(jnp.bfloat16), TP, 5).astype(jnp.float32)
    return (hidden_state + expert_mix).astype(jnp.bfloat16)


def solution(mesh):
    return jax.shard_map(
        per_device,
        mesh=mesh,
        in_specs=(
            P("req", "tp"),
            P("req", None, None, "tp"),
            P("req", None),
            P("req"),
            P("req", None),
            P("req", "tp"),
            P(),
            P(),
            P("tp", None, "req"),
            P("tp", None, "req"),
            P("tp", "req", None),
            P("req", None),
        ),
        out_specs=P("req", None),
        check_vma=False,
    )
```

```python
import functools

import jax
import jax.numpy as jnp
from jax import lax
from jax.experimental import pallas as pl
from jax.experimental.pallas import tpu as pltpu
from jax.sharding import PartitionSpec as P

D = 4096
HD = 128
EXPERTS = 8
CAP = 8
TP = 8

MESH = pl.DeviceIdType.MESH
NY = 8
NZ = 8


def place_of(me, swap):
    y, z = me // NZ, me % NZ
    return z + swap * (y - z), y + swap * (z - y)


def index_of(a, b, swap):
    return (b + swap * (a - b)) * NZ + a + swap * (b - a)


def gather_kernel(split, x_ref, out_ref, own_sem, send_sem, recv_sem):
    me = lax.axis_index("req")
    swap = lax.axis_index("tp") % 2
    sign = 1 - 2 * swap
    y, z = me // NZ, me % NZ

    def at_z(step):
        return (z + sign * step + 2 * NZ) % NZ

    def at_y(step):
        return (y + sign * step + 2 * NY) % NY

    neighbours = [
        {1: y * NZ + at_z(1), -1: y * NZ + at_z(-1)},
        {1: at_y(1) * NZ + z, -1: at_y(-1) * NZ + z},
    ]
    barrier = pltpu.get_barrier_semaphore()
    for axis in range(2):
        for way in (1, -1):
            pl.semaphore_signal(
                barrier, inc=1, device_id={"req": neighbours[axis][way]}, device_id_type=MESH
            )
    pl.semaphore_wait(barrier, 4)
    own = pltpu.make_async_copy(x_ref, out_ref.at[y, z], own_sem)
    own.start()
    rows, columns = x_ref.shape
    if split == 0:
        halves = [
            (pl.ds(0, rows // 2), slice(None)),
            (pl.ds(rows // 2, rows // 2), slice(None)),
        ]
    else:
        halves = [
            (slice(None), pl.ds(0, columns // 2)),
            (slice(None), pl.ds(columns // 2, columns // 2)),
        ]

    plan = []
    for half in range(2):
        for way, steps in ((1, 4), (-1, 3)):
            for step in range(steps):
                needs = (half, 1, way, 0, step - 1) if step else None
                plan.append((step, 0, (half, 1, way, 0, step), needs))
                for far in (0, -1, 1, -2, 2, -3, 3, -4):
                    if step:
                        needs = (half, 2, way, far, step - 1)
                    elif far:
                        needs = (half, 1, 1 if far < 0 else -1, 0, abs(far) - 1)
                    else:
                        needs = None
                    plan.append((abs(far) + step, 1, (half, 2, way, far, step), needs))
    plan.sort(key=lambda entry: entry[:2])
    copies, landed = {}, set()
    for entry, (_, _, key, needs) in enumerate(plan):
        half, phase, way, far, step = key
        if needs is not None and needs not in landed:
            copies[needs].wait_recv()
            landed.add(needs)
        one, two = (-way * step, 0) if phase == 1 else (far, -way * step)
        where = (at_y(two), at_z(one)) if half == 0 else (at_y(one), at_z(two))
        region = out_ref.at[where + halves[half]]
        first = step == 0 and far == 0
        copy = pltpu.make_async_remote_copy(
            src_ref=x_ref.at[halves[half]] if first else region,
            dst_ref=region,
            send_sem=send_sem.at[entry],
            recv_sem=recv_sem.at[entry],
            device_id={"req": neighbours[(half + phase - 1) % 2][way]},
            device_id_type=MESH,
        )
        copy.start()
        copies[key] = copy
    for key, copy in copies.items():
        if key not in landed:
            copy.wait_recv()
    own.wait()
    for copy in copies.values():
        copy.wait_send()


def gather(chunk, split, number):
    rows, columns = chunk.shape
    return pl.pallas_call(
        functools.partial(gather_kernel, split),
        out_shape=jax.ShapeDtypeStruct((NY, NZ, rows, columns), chunk.dtype),
        in_specs=[pl.BlockSpec(memory_space=pltpu.VMEM)],
        out_specs=pl.BlockSpec(memory_space=pl.ANY),
        scratch_shapes=[
            pltpu.SemaphoreType.DMA(()),
            pltpu.SemaphoreType.DMA((126,)),
            pltpu.SemaphoreType.DMA((126,)),
        ],
        compiler_params=pltpu.CompilerParams(collective_id=number, has_side_effects=True),
    )(chunk)


def project_kernel(
    n, x_ref, w_ref, down_ref, out_ref, laid_ref,
    rows_all, w_all, partial, landing, parts, own,
    own_sem, row_send, row_recv, ring_send, ring_recv, back_send, back_recv,
    sum_send, sum_recv, lay_send, lay_recv,
):
    me = lax.axis_index("req")
    t = lax.axis_index("tp")
    swap = t % 2
    a, b = place_of(me, swap)
    y, z = me // NZ, me % NZ
    barrier = pltpu.get_barrier_semaphore()
    for step in range(1, NY):
        for peer in (
            {"req": y * NZ + (z + step) % NZ},
            {"req": ((y + step) % NY) * NZ + z},
            {"tp": (t + step) % n},
        ):
            pl.semaphore_signal(barrier, inc=1, device_id=peer, device_id_type=MESH)
    pl.semaphore_wait(barrier, 2 * (NY - 1) + n - 1)

    laid = []

    def lay(far):
        for step in range(1, NY):
            to = (b + step) % NY
            width = pl.ds(pl.multiple_of(index_of(far, to, swap) * 128, 128), 128)
            copy = pltpu.make_async_remote_copy(
                src_ref=down_ref.at[:, width],
                dst_ref=laid_ref.at[b, :, pl.ds(far * 128, 128)],
                send_sem=lay_send.at[step - 1, far],
                recv_sem=lay_recv.at[step - 1, far],
                device_id={"req": index_of(a, to, swap)},
                device_id_type=MESH,
            )
            copy.start()
            laid.append(copy)

    sign = 1 - 2 * swap
    ring = {}
    spread = []
    for step in range(4):
        for way in (1, -1):
            if way == -1 and step == 3:
                continue
            if step:
                ring[way, step - 1].wait_recv()
            region = w_all.at[(z - sign * way * step + 2 * NZ) % NZ]
            copy = pltpu.make_async_remote_copy(
                src_ref=region if step else w_ref,
                dst_ref=region,
                send_sem=ring_send.at[(1 - way) // 2, step],
                recv_sem=ring_recv.at[(1 - way) // 2, step],
                device_id={"req": y * NZ + (z + sign * way + NZ) % NZ},
                device_id_type=MESH,
            )
            copy.start()
            ring[way, step] = copy
        if step == 0:
            for far in range(1, NY):
                copy = pltpu.make_async_remote_copy(
                    src_ref=x_ref,
                    dst_ref=rows_all.at[y],
                    send_sem=row_send.at[far - 1],
                    recv_sem=row_recv.at[far - 1],
                    device_id={"req": ((y + far) % NY) * NZ + z},
                    device_id_type=MESH,
                )
                copy.start()
                spread.append(copy)
            rows_all[y] = x_ref[...]
            w_all[z] = w_ref[...]
        lay(step)
    for far in range(NY):
        width = pl.ds(pl.multiple_of(index_of(far, b, swap) * 128, 128), 128)
        laid_ref[b, :, pl.ds(far * 128, 128)] = down_ref[:, width]
    ring[1, 3].wait_recv()
    ring[-1, 2].wait_recv()
    for copy in spread:
        copy.wait_recv()
    depth = x_ref.shape[1]
    product = lax.dot_general(
        rows_all[...].reshape(-1, depth),
        w_all[...].reshape(-1, depth),
        (((1,), (1,)), ((), ())),
        preferred_element_type=jnp.float32,
    )
    partial[...] = product.reshape(partial.shape)
    back = []
    for far in range(1, NY):
        to = (y + far) % NY
        copy = pltpu.make_async_remote_copy(
            src_ref=partial.at[to],
            dst_ref=landing.at[y],
            send_sem=back_send.at[far - 1],
            recv_sem=back_recv.at[far - 1],
            device_id={"req": to * NZ + z},
            device_id_type=MESH,
        )
        copy.start()
        back.append(copy)
    landing[y] = partial[y]
    for far in range(4, NY):
        lay(far)
    for copy in back:
        copy.wait_recv()

    def columns(index):
        return pl.ds(pl.multiple_of(index * landing.shape[2], landing.shape[2]), landing.shape[2])

    scatter = []
    for step in range(1, n):
        peer = (t + step) % n
        copy = pltpu.make_async_remote_copy(
            src_ref=landing.at[peer],
            dst_ref=parts.at[step - 1],
            send_sem=sum_send.at[0, step - 1],
            recv_sem=sum_recv.at[0, step - 1],
            device_id={"tp": peer},
            device_id_type=MESH,
        )
        copy.start()
        scatter.append(copy)
    total = landing[t]
    for step in range(1, n):
        scatter[step - 1].wait_recv()
        total = total + parts[step - 1]
    own[...] = total
    share = []
    for step in range(1, n):
        copy = pltpu.make_async_remote_copy(
            src_ref=own,
            dst_ref=out_ref.at[:, columns(t)],
            send_sem=sum_send.at[1, step - 1],
            recv_sem=sum_recv.at[1, step - 1],
            device_id={"tp": (t + step) % n},
            device_id_type=MESH,
        )
        copy.start()
        share.append(copy)
    mine = pltpu.make_async_copy(own, out_ref.at[:, columns(t)], own_sem)
    mine.start()
    for copy in share:
        copy.wait_recv()
    for copy in laid:
        copy.wait_recv()
    for copy in [*ring.values(), *spread, *back, *scatter, *share, *laid]:
        copy.wait_send()
    mine.wait()


def project(attended, weight, down, n, number):
    rows, depth = attended.shape
    outs = weight.shape[0]
    wide = NZ * outs
    vmem = pl.BlockSpec(memory_space=pltpu.VMEM)
    dma = pltpu.SemaphoreType.DMA
    return pl.pallas_call(
        functools.partial(project_kernel, n),
        out_shape=[
            jax.ShapeDtypeStruct((rows, NY * wide), jnp.float32),
            jax.ShapeDtypeStruct((NY, down.shape[0], down.shape[1] // NY), down.dtype),
        ],
        in_specs=[vmem] * 3,
        out_specs=[vmem] * 2,
        scratch_shapes=[
            pltpu.VMEM((NY, rows, depth), attended.dtype),
            pltpu.VMEM((NZ, outs, depth), weight.dtype),
            pltpu.VMEM((NY, rows, wide), jnp.float32),
            pltpu.VMEM((NY, rows, wide), jnp.float32),
            pltpu.VMEM((n - 1, rows, wide), jnp.float32),
            pltpu.VMEM((rows, wide), jnp.float32),
            dma(()),
            dma((7,)), dma((7,)),
            dma((2, 4)), dma((2, 4)),
            dma((7,)), dma((7,)),
            dma((2, n - 1)), dma((2, n - 1)),
            dma((7, 8)), dma((7, 8)),
        ],
        compiler_params=pltpu.CompilerParams(collective_id=number, has_side_effects=True),
    )(attended, weight, down)


def down_kernel(x_ref, laid_ref, out_ref, units, partial, landing, ring_send, ring_recv, send_sem, recv_sem):
    me = lax.axis_index("req")
    swap = lax.axis_index("tp") % 2
    a, b = place_of(me, swap)
    groups = NY * NZ
    barrier = pltpu.get_barrier_semaphore()

    @pl.loop(1, groups)
    def _(step):
        pl.semaphore_signal(
            barrier,
            inc=1,
            device_id={"req": (me + step) % groups},
            device_id_type=MESH,
        )

    pl.semaphore_wait(barrier, groups - 1)

    def block(step):
        return pl.ds(pl.multiple_of(((a + step + NZ) % NZ) * 128, 128), 128)

    copies = {}
    for step in range(4):
        for way in (1, -1):
            if way == -1 and step == 3:
                continue
            if step:
                copies[way, step - 1].wait_recv()
            region = units.at[:, block(-way * step)]
            copy = pltpu.make_async_remote_copy(
                src_ref=region if step else x_ref,
                dst_ref=region,
                send_sem=ring_send.at[(1 - way) // 2, step],
                recv_sem=ring_recv.at[(1 - way) // 2, step],
                device_id={"req": index_of((a + way + NZ) % NZ, b, swap)},
                device_id_type=MESH,
            )
            copy.start()
            copies[way, step] = copy
        if step == 0:
            units[:, block(0)] = x_ref[...]
    copies[1, 3].wait_recv()
    copies[-1, 2].wait_recv()
    weights = laid_ref[...].reshape(laid_ref.shape[0] * laid_ref.shape[1], laid_ref.shape[2])
    product = lax.dot_general(
        units[...], weights, (((1,), (1,)), ((), ())), preferred_element_type=jnp.float32
    )
    partial[...] = product.astype(partial.dtype).reshape(partial.shape)

    def message(step):
        to = (me + step) % groups
        return pltpu.make_async_remote_copy(
            src_ref=partial.at[to],
            dst_ref=landing.at[b * NZ + a],
            send_sem=send_sem.at[step - 1],
            recv_sem=recv_sem.at[step - 1],
            device_id={"req": to},
            device_id_type=MESH,
        )

    @pl.loop(1, groups)
    def _(step):
        message(step).start()

    landing[b * NZ + a] = partial[me]

    @pl.loop(1, groups)
    def _(step):
        message(step).wait_recv()

    total = landing[pl.ds(0, NZ)].astype(jnp.float32)
    for row in range(1, NY):
        total = total + landing[pl.ds(row * NZ, NZ)].astype(jnp.float32)
    out_ref[...] = total

    @pl.loop(1, groups)
    def _(step):
        message(step).wait_send()

    for copy in copies.values():
        copy.wait_send()


def down_and_return(activated, laid, number):
    rows, width = activated.shape
    outs = laid.shape[0] * laid.shape[1]
    groups = NY * NZ
    return pl.pallas_call(
        down_kernel,
        out_shape=jax.ShapeDtypeStruct((NZ, rows // groups, outs), jnp.float32),
        in_specs=[pl.BlockSpec(memory_space=pltpu.VMEM)] * 2,
        out_specs=pl.BlockSpec(memory_space=pltpu.VMEM),
        scratch_shapes=[
            pltpu.VMEM((rows, NZ * width), activated.dtype),
            pltpu.VMEM((groups, rows // groups, outs), jnp.bfloat16),
            pltpu.VMEM((groups, rows // groups, outs), jnp.bfloat16),
            pltpu.SemaphoreType.DMA((2, 4)),
            pltpu.SemaphoreType.DMA((2, 4)),
            pltpu.SemaphoreType.DMA((groups - 1,)),
            pltpu.SemaphoreType.DMA((groups - 1,)),
        ],
        compiler_params=pltpu.CompilerParams(collective_id=number, has_side_effects=True),
    )(activated, laid)


def total_kernel(n, x_ref, out_ref, parts, own, own_sem, send_sem, recv_sem):
    me = lax.axis_index("tp")
    width = x_ref.shape[1] // n
    barrier = pltpu.get_barrier_semaphore()
    for step in range(1, n):
        pl.semaphore_signal(
            barrier, inc=1, device_id={"tp": (me + step) % n}, device_id_type=MESH
        )
    pl.semaphore_wait(barrier, n - 1)

    def columns(index):
        return pl.ds(pl.multiple_of(index * width, width), width)

    scatter = []
    for step in range(1, n):
        peer = (me + step) % n
        copy = pltpu.make_async_remote_copy(
            src_ref=x_ref.at[:, columns(peer)],
            dst_ref=parts.at[step - 1],
            send_sem=send_sem.at[0, step - 1],
            recv_sem=recv_sem.at[0, step - 1],
            device_id={"tp": peer},
            device_id_type=MESH,
        )
        copy.start()
        scatter.append(copy)
    total = x_ref[:, columns(me)].astype(jnp.float32)
    for step in range(1, n):
        scatter[step - 1].wait_recv()
        total = total + parts[step - 1].astype(jnp.float32)
    own[...] = total.astype(own.dtype)
    spread = []
    for step in range(1, n):
        peer = (me + step) % n
        copy = pltpu.make_async_remote_copy(
            src_ref=own,
            dst_ref=out_ref.at[:, columns(me)],
            send_sem=send_sem.at[1, step - 1],
            recv_sem=recv_sem.at[1, step - 1],
            device_id={"tp": peer},
            device_id_type=MESH,
        )
        copy.start()
        spread.append(copy)
    mine = pltpu.make_async_copy(own, out_ref.at[:, columns(me)], own_sem)
    mine.start()
    for copy in scatter:
        copy.wait_send()
    for copy in spread:
        copy.wait_recv()
    for copy in spread:
        copy.wait_send()
    mine.wait()


def total_over_tp(x, n, number):
    rows, columns = x.shape
    return pl.pallas_call(
        functools.partial(total_kernel, n),
        out_shape=jax.ShapeDtypeStruct(x.shape, x.dtype),
        in_specs=[pl.BlockSpec(memory_space=pltpu.VMEM)],
        out_specs=pl.BlockSpec(memory_space=pltpu.VMEM),
        scratch_shapes=[
            pltpu.VMEM((n - 1, rows, columns // n), x.dtype),
            pltpu.VMEM((rows, columns // n), x.dtype),
            pltpu.SemaphoreType.DMA(()),
            pltpu.SemaphoreType.DMA((2, n - 1)),
            pltpu.SemaphoreType.DMA((2, n - 1)),
        ],
        compiler_params=pltpu.CompilerParams(collective_id=number, has_side_effects=True),
    )(x)


def attend(queries, pool, table, lengths):
    row_count = queries.shape[0]
    slot_count = lengths.shape[0]
    page_size = pool.shape[2]
    kv_width = pool.shape[3] // HD
    group_size = queries.shape[1] // pool.shape[3]
    context = table.shape[1] * page_size
    prefill = row_count - slot_count + 1
    row_index = jnp.arange(row_count, dtype=jnp.int32)
    row_slot = jnp.maximum(row_index - prefill + 1, 0)
    slot_match = row_slot[:, None] == jnp.arange(slot_count, dtype=jnp.int32)[None, :]
    row_length = jnp.sum(jnp.where(slot_match, lengths[None, :], 0), axis=1)
    row_position = jnp.where(row_index < prefill, row_length - prefill + row_index, row_length - 1)
    pages = jnp.take(pool, table.reshape(-1), axis=0)
    keys = pages[:, 0].reshape(slot_count * context, kv_width, HD)
    values = pages[:, 1].reshape(slot_count * context, kv_width, HD)
    key_index = jnp.arange(slot_count * context, dtype=jnp.int32)
    valid = ((key_index // context)[None, :] == row_slot[:, None]) & (
        (key_index % context)[None, :] <= row_position[:, None]
    )
    shaped = queries.reshape(row_count, kv_width, group_size, HD)
    scores = jnp.einsum("rkgd,skd->rkgs", shaped, keys, preferred_element_type=jnp.float32) * (
        1.0 / HD**0.5
    )
    usable = valid[:, None, None, :]
    masked = jnp.where(usable, scores, -1e30)
    peak = jnp.max(masked, axis=3, keepdims=True)
    weights = jnp.where(usable, jnp.exp(masked - peak), 0.0)
    probs = (weights / jnp.sum(weights, axis=3, keepdims=True)).astype(jnp.bfloat16)
    mixed = jnp.einsum("rkgs,skd->rkgd", probs, values, preferred_element_type=jnp.float32)
    return mixed.reshape(row_count, kv_width * group_size * HD).astype(jnp.bfloat16)


def per_device(
    queries,
    kv_cache,
    page_table,
    cache_lengths,
    residual,
    out_weight,
    norm_gain,
    router,
    gate_weight,
    up_weight,
    down_weight,
    expert_ids,
):
    attended = attend(queries, kv_cache, page_table, cache_lengths)
    projected, laid = project(attended, out_weight, down_weight[0], TP, 1)
    hidden_state = residual.astype(jnp.float32) + projected
    inverse = lax.rsqrt(jnp.mean(hidden_state * hidden_state, axis=1, keepdims=True) + 1e-05)
    normed = (hidden_state * inverse * norm_gain[None, :]).astype(jnp.bfloat16)
    logits = jnp.dot(normed, router, preferred_element_type=jnp.float32)
    expert_range = jnp.arange(EXPERTS, dtype=jnp.int32)
    chosen = jnp.sum(
        jnp.where(expert_ids[:, :, None] == expert_range[None, None, :], logits[:, None, :], 0.0),
        axis=2,
    )
    first = jax.nn.sigmoid(chosen[:, 0] - chosen[:, 1])
    mixing = jnp.stack([first, 1.0 - first], axis=1).reshape(-1)
    flat = expert_ids.reshape(-1)
    onehot = (flat[:, None] == expert_range[None, :]).astype(jnp.int32)
    before = jnp.cumsum(onehot, axis=0) - onehot
    slot = jnp.sum(before * onehot, axis=1)
    local_experts = gate_weight.shape[0]
    owned = lax.axis_index("tp") * local_experts + jnp.arange(local_experts, dtype=jnp.int32)
    capacity_range = jnp.arange(CAP, dtype=jnp.int32)
    select = (flat[None, None, :] == owned[:, None, None]) & (
        slot[None, None, :] == capacity_range[None, :, None]
    )
    repeated = jnp.repeat(normed, 2, axis=0)
    dispatched = jnp.einsum(
        "ecr,rd->ecd", select.astype(jnp.bfloat16), repeated, preferred_element_type=jnp.float32
    ).astype(jnp.bfloat16)[0]
    shard_piece = gather(dispatched, 1, 3).reshape(-1, D)
    gate = jnp.dot(shard_piece, gate_weight[0], preferred_element_type=jnp.float32)
    upward = jnp.dot(shard_piece, up_weight[0], preferred_element_type=jnp.float32)
    activated = (jax.nn.silu(gate) * upward).astype(jnp.bfloat16)
    pieces = down_and_return(activated, laid, 4).reshape(NZ, CAP, NY, -1)
    outputs = jnp.where(
        lax.axis_index("tp") % 2 == 0,
        jnp.transpose(pieces, (1, 2, 0, 3)),
        jnp.transpose(pieces, (1, 0, 2, 3)),
    ).reshape(local_experts, CAP, D)
    gathered = jnp.einsum("ecr,ecd->rd", select.astype(jnp.float32), outputs)
    weighted = gathered * mixing[:, None]
    local_mix = jnp.sum(weighted.reshape(residual.shape[0], 2, D), axis=1)
    expert_mix = total_over_tp(local_mix.astype(jnp.bfloat16), TP, 5).astype(jnp.float32)
    return (hidden_state + expert_mix).astype(jnp.bfloat16)


def solution(mesh):
    return jax.shard_map(
        per_device,
        mesh=mesh,
        in_specs=(
            P("req", "tp"),
            P("req", None, None, "tp"),
            P("req", None),
            P("req"),
            P("req", None),
            P("req", "tp"),
            P(),
            P(),
            P("tp", None, "req"),
            P("tp", None, "req"),
            P("tp", "req", None),
            P("req", None),
        ),
        out_specs=P("req", None),
        check_vma=False,
    )
```

```python
import functools

import jax
import jax.numpy as jnp
from jax import lax
from jax.experimental import pallas as pl
from jax.experimental.pallas import tpu as pltpu
from jax.sharding import PartitionSpec as P

D = 4096
HD = 128
EXPERTS = 8
CAP = 8
TP = 8

MESH = pl.DeviceIdType.MESH
NY = 8
NZ = 8


def place_of(me, swap):
    y, z = me // NZ, me % NZ
    return z + swap * (y - z), y + swap * (z - y)


def index_of(a, b, swap):
    return (b + swap * (a - b)) * NZ + a + swap * (b - a)


def project_kernel(
    n, x_ref, w_ref, down_ref, out_ref, laid_ref,
    rows_all, w_all, partial, landing, parts, own,
    own_sem, row_send, row_recv, ring_send, ring_recv, back_send, back_recv,
    sum_send, sum_recv, lay_send, lay_recv,
):
    me = lax.axis_index("req")
    t = lax.axis_index("tp")
    swap = t % 2
    a, b = place_of(me, swap)
    y, z = me // NZ, me % NZ
    barrier = pltpu.get_barrier_semaphore()
    for step in range(1, NY):
        for peer in (
            {"req": y * NZ + (z + step) % NZ},
            {"req": ((y + step) % NY) * NZ + z},
            {"tp": (t + step) % n},
        ):
            pl.semaphore_signal(barrier, inc=1, device_id=peer, device_id_type=MESH)
    pl.semaphore_wait(barrier, 2 * (NY - 1) + n - 1)

    laid = []

    def lay(far):
        for step in range(1, NY):
            to = (b + step) % NY
            width = pl.ds(pl.multiple_of(index_of(far, to, swap) * 128, 128), 128)
            copy = pltpu.make_async_remote_copy(
                src_ref=down_ref.at[:, width],
                dst_ref=laid_ref.at[b, :, pl.ds(far * 128, 128)],
                send_sem=lay_send.at[step - 1, far],
                recv_sem=lay_recv.at[step - 1, far],
                device_id={"req": index_of(a, to, swap)},
                device_id_type=MESH,
            )
            copy.start()
            laid.append(copy)

    sign = 1 - 2 * swap
    ring = {}
    spread = []
    for step in range(4):
        for way in (1, -1):
            if way == -1 and step == 3:
                continue
            if step:
                ring[way, step - 1].wait_recv()
            region = w_all.at[(z - sign * way * step + 2 * NZ) % NZ]
            copy = pltpu.make_async_remote_copy(
                src_ref=region if step else w_ref,
                dst_ref=region,
                send_sem=ring_send.at[(1 - way) // 2, step],
                recv_sem=ring_recv.at[(1 - way) // 2, step],
                device_id={"req": y * NZ + (z + sign * way + NZ) % NZ},
                device_id_type=MESH,
            )
            copy.start()
            ring[way, step] = copy
        if step == 0:
            for far in range(1, NY):
                copy = pltpu.make_async_remote_copy(
                    src_ref=x_ref,
                    dst_ref=rows_all.at[y],
                    send_sem=row_send.at[far - 1],
                    recv_sem=row_recv.at[far - 1],
                    device_id={"req": ((y + far) % NY) * NZ + z},
                    device_id_type=MESH,
                )
                copy.start()
                spread.append(copy)
            rows_all[y] = x_ref[...]
            w_all[z] = w_ref[...]
    ring[1, 3].wait_recv()
    ring[-1, 2].wait_recv()
    for copy in spread:
        copy.wait_recv()
    depth = x_ref.shape[1]
    product = lax.dot_general(
        rows_all[...].reshape(-1, depth),
        w_all[...].reshape(-1, depth),
        (((1,), (1,)), ((), ())),
        preferred_element_type=jnp.float32,
    )
    partial[...] = product.reshape(partial.shape)
    back = []
    for far in range(1, NY):
        to = (y + far) % NY
        copy = pltpu.make_async_remote_copy(
            src_ref=partial.at[to],
            dst_ref=landing.at[y],
            send_sem=back_send.at[far - 1],
            recv_sem=back_recv.at[far - 1],
            device_id={"req": to * NZ + z},
            device_id_type=MESH,
        )
        copy.start()
        back.append(copy)
    landing[y] = partial[y]
    for far in range(NY):
        lay(far)
    for far in range(NY):
        width = pl.ds(pl.multiple_of(index_of(far, b, swap) * 128, 128), 128)
        laid_ref[b, :, pl.ds(far * 128, 128)] = down_ref[:, width]
    for copy in back:
        copy.wait_recv()

    def columns(index):
        return pl.ds(pl.multiple_of(index * landing.shape[2], landing.shape[2]), landing.shape[2])

    scatter = []
    for step in range(1, n):
        peer = (t + step) % n
        copy = pltpu.make_async_remote_copy(
            src_ref=landing.at[peer],
            dst_ref=parts.at[step - 1],
            send_sem=sum_send.at[0, step - 1],
            recv_sem=sum_recv.at[0, step - 1],
            device_id={"tp": peer},
            device_id_type=MESH,
        )
        copy.start()
        scatter.append(copy)
    total = landing[t]
    for step in range(1, n):
        scatter[step - 1].wait_recv()
        total = total + parts[step - 1]
    own[...] = total
    share = []
    for step in range(1, n):
        copy = pltpu.make_async_remote_copy(
            src_ref=own,
            dst_ref=out_ref.at[:, columns(t)],
            send_sem=sum_send.at[1, step - 1],
            recv_sem=sum_recv.at[1, step - 1],
            device_id={"tp": (t + step) % n},
            device_id_type=MESH,
        )
        copy.start()
        share.append(copy)
    mine = pltpu.make_async_copy(own, out_ref.at[:, columns(t)], own_sem)
    mine.start()
    for copy in share:
        copy.wait_recv()
    for copy in laid:
        copy.wait_recv()
    for copy in [*ring.values(), *spread, *back, *scatter, *share, *laid]:
        copy.wait_send()
    mine.wait()


def project(attended, weight, down, n, number):
    rows, depth = attended.shape
    outs = weight.shape[0]
    wide = NZ * outs
    vmem = pl.BlockSpec(memory_space=pltpu.VMEM)
    dma = pltpu.SemaphoreType.DMA
    return pl.pallas_call(
        functools.partial(project_kernel, n),
        out_shape=[
            jax.ShapeDtypeStruct((rows, NY * wide), jnp.float32),
            jax.ShapeDtypeStruct((NY, down.shape[0], down.shape[1] // NY), down.dtype),
        ],
        in_specs=[vmem] * 3,
        out_specs=[vmem] * 2,
        scratch_shapes=[
            pltpu.VMEM((NY, rows, depth), attended.dtype),
            pltpu.VMEM((NZ, outs, depth), weight.dtype),
            pltpu.VMEM((NY, rows, wide), jnp.float32),
            pltpu.VMEM((NY, rows, wide), jnp.float32),
            pltpu.VMEM((n - 1, rows, wide), jnp.float32),
            pltpu.VMEM((rows, wide), jnp.float32),
            dma(()),
            dma((7,)), dma((7,)),
            dma((2, 4)), dma((2, 4)),
            dma((7,)), dma((7,)),
            dma((2, n - 1)), dma((2, n - 1)),
            dma((7, 8)), dma((7, 8)),
        ],
        compiler_params=pltpu.CompilerParams(collective_id=number, has_side_effects=True),
    )(attended, weight, down)


def moe_kernel(
    x_ref, gate_ref, up_ref, laid_ref, out_ref,
    held, both, products, units, partial, landing,
    own_sem, hop_send, hop_recv, ring_send, ring_recv, send_sem, recv_sem,
):
    me = lax.axis_index("req")
    swap = lax.axis_index("tp") % 2
    sign = 1 - 2 * swap
    y, z = me // NZ, me % NZ
    a, b = place_of(me, swap)

    def at_z(step):
        return (z + sign * step + 2 * NZ) % NZ

    def at_y(step):
        return (y + sign * step + 2 * NY) % NY

    neighbours = [
        {1: y * NZ + at_z(1), -1: y * NZ + at_z(-1)},
        {1: at_y(1) * NZ + z, -1: at_y(-1) * NZ + z},
    ]
    groups = NY * NZ
    barrier = pltpu.get_barrier_semaphore()

    @pl.loop(1, groups)
    def _(step):
        pl.semaphore_signal(
            barrier, inc=1, device_id={"req": (me + step) % groups}, device_id_type=MESH
        )

    both[:, : gate_ref.shape[1]] = gate_ref[...]
    both[:, gate_ref.shape[1] :] = up_ref[...]
    products[...] = jnp.zeros_like(products)
    pl.semaphore_wait(barrier, groups - 1)
    own = pltpu.make_async_copy(x_ref, held.at[y, z], own_sem)
    own.start()
    columns = x_ref.shape[1]
    halves = [
        (slice(None), pl.ds(0, columns // 2)),
        (slice(None), pl.ds(columns // 2, columns // 2)),
    ]

    plan = []
    for half in range(2):
        for way, steps in ((1, 4), (-1, 3)):
            for step in range(steps):
                needs = (half, 1, way, 0, step - 1) if step else None
                plan.append((step, 0, (half, 1, way, 0, step), needs))
                for far in (0, -1, 1, -2, 2, -3, 3, -4):
                    if step:
                        needs = (half, 2, way, far, step - 1)
                    elif far:
                        needs = (half, 1, 1 if far < 0 else -1, 0, abs(far) - 1)
                    else:
                        needs = None
                    plan.append((abs(far) + step, 1, (half, 2, way, far, step), needs))
    plan.sort(key=lambda entry: entry[:2])
    hops, landed = {}, set()
    for entry, (_, _, key, needs) in enumerate(plan):
        half, phase, way, far, step = key
        if needs is not None and needs not in landed:
            hops[needs].wait_recv()
            landed.add(needs)
        one, two = (-way * step, 0) if phase == 1 else (far, -way * step)
        where = (at_y(two), at_z(one)) if half == 0 else (at_y(one), at_z(two))
        region = held.at[where + halves[half]]
        first = step == 0 and far == 0
        copy = pltpu.make_async_remote_copy(
            src_ref=x_ref.at[halves[half]] if first else region,
            dst_ref=region,
            send_sem=hop_send.at[entry],
            recv_sem=hop_recv.at[entry],
            device_id={"req": neighbours[(half + phase - 1) % 2][way]},
            device_id_type=MESH,
        )
        copy.start()
        hops[key] = copy
    for key, copy in hops.items():
        if key not in landed:
            copy.wait_recv()
    own.wait()
    depth = 512
    width = gate_ref.shape[1]

    @pl.loop(0, columns // depth)
    def _(step):
        span = pl.ds(pl.multiple_of(step * depth, depth), depth)
        block = held[:, :, :, span].reshape(products.shape[0], depth)
        products[...] += jnp.dot(block, both[span, :], preferred_element_type=jnp.float32)

    gate = products[:, :width]
    active = (gate / (1.0 + jnp.exp(-gate)) * products[:, width:]).astype(units.dtype)

    def block(step):
        return pl.ds(pl.multiple_of(((a + step + NZ) % NZ) * 128, 128), 128)

    units[:, block(0)] = active
    copies = {}
    for step in range(4):
        for way in (1, -1):
            if way == -1 and step == 3:
                continue
            if step:
                copies[way, step - 1].wait_recv()
            region = units.at[:, block(-way * step)]
            copy = pltpu.make_async_remote_copy(
                src_ref=region,
                dst_ref=region,
                send_sem=ring_send.at[(1 - way) // 2, step],
                recv_sem=ring_recv.at[(1 - way) // 2, step],
                device_id={"req": index_of((a + way + NZ) % NZ, b, swap)},
                device_id_type=MESH,
            )
            copy.start()
            copies[way, step] = copy
    copies[1, 3].wait_recv()
    copies[-1, 2].wait_recv()
    weights = laid_ref[...].reshape(laid_ref.shape[0] * laid_ref.shape[1], laid_ref.shape[2])
    product = lax.dot_general(
        units[...], weights, (((1,), (1,)), ((), ())), preferred_element_type=jnp.float32
    )
    partial[...] = product.astype(partial.dtype).reshape(partial.shape)

    def message(step):
        to = (me + step) % groups
        return pltpu.make_async_remote_copy(
            src_ref=partial.at[to],
            dst_ref=landing.at[b * NZ + a],
            send_sem=send_sem.at[step - 1],
            recv_sem=recv_sem.at[step - 1],
            device_id={"req": to},
            device_id_type=MESH,
        )

    @pl.loop(1, groups)
    def _(step):
        message(step).start()

    landing[b * NZ + a] = partial[me]

    @pl.loop(1, groups)
    def _(step):
        message(step).wait_recv()

    total = landing[pl.ds(0, NZ)].astype(jnp.float32)
    for row in range(1, NY):
        total = total + landing[pl.ds(row * NZ, NZ)].astype(jnp.float32)
    out_ref[...] = total

    @pl.loop(1, groups)
    def _(step):
        message(step).wait_send()

    for copy in [*hops.values(), *copies.values()]:
        copy.wait_send()


def run_expert(rows, gate, up, laid, number):
    slots, columns = rows.shape
    width = gate.shape[1]
    outs = laid.shape[0] * laid.shape[1]
    groups = NY * NZ
    vmem = pl.BlockSpec(memory_space=pltpu.VMEM)
    dma = pltpu.SemaphoreType.DMA
    return pl.pallas_call(
        moe_kernel,
        out_shape=jax.ShapeDtypeStruct((NZ, slots, outs), jnp.float32),
        in_specs=[vmem] * 4,
        out_specs=vmem,
        scratch_shapes=[
            pltpu.VMEM((NY, NZ, slots, columns), rows.dtype),
            pltpu.VMEM((columns, 2 * width), gate.dtype),
            pltpu.VMEM((groups * slots, 2 * width), jnp.float32),
            pltpu.VMEM((groups * slots, NZ * width), rows.dtype),
            pltpu.VMEM((groups, slots, outs), jnp.bfloat16),
            pltpu.VMEM((groups, slots, outs), jnp.bfloat16),
            dma(()),
            dma((126,)), dma((126,)),
            dma((2, 4)), dma((2, 4)),
            dma((groups - 1,)), dma((groups - 1,)),
        ],
        compiler_params=pltpu.CompilerParams(collective_id=number, has_side_effects=True),
    )(rows, gate, up, laid)


def total_kernel(n, x_ref, out_ref, parts, own, own_sem, send_sem, recv_sem):
    me = lax.axis_index("tp")
    width = x_ref.shape[1] // n
    barrier = pltpu.get_barrier_semaphore()
    for step in range(1, n):
        pl.semaphore_signal(
            barrier, inc=1, device_id={"tp": (me + step) % n}, device_id_type=MESH
        )
    pl.semaphore_wait(barrier, n - 1)

    def columns(index):
        return pl.ds(pl.multiple_of(index * width, width), width)

    scatter = []
    for step in range(1, n):
        peer = (me + step) % n
        copy = pltpu.make_async_remote_copy(
            src_ref=x_ref.at[:, columns(peer)],
            dst_ref=parts.at[step - 1],
            send_sem=send_sem.at[0, step - 1],
            recv_sem=recv_sem.at[0, step - 1],
            device_id={"tp": peer},
            device_id_type=MESH,
        )
        copy.start()
        scatter.append(copy)
    total = x_ref[:, columns(me)].astype(jnp.float32)
    for step in range(1, n):
        scatter[step - 1].wait_recv()
        total = total + parts[step - 1].astype(jnp.float32)
    own[...] = total.astype(own.dtype)
    spread = []
    for step in range(1, n):
        peer = (me + step) % n
        copy = pltpu.make_async_remote_copy(
            src_ref=own,
            dst_ref=out_ref.at[:, columns(me)],
            send_sem=send_sem.at[1, step - 1],
            recv_sem=recv_sem.at[1, step - 1],
            device_id={"tp": peer},
            device_id_type=MESH,
        )
        copy.start()
        spread.append(copy)
    mine = pltpu.make_async_copy(own, out_ref.at[:, columns(me)], own_sem)
    mine.start()
    for copy in scatter:
        copy.wait_send()
    for copy in spread:
        copy.wait_recv()
    for copy in spread:
        copy.wait_send()
    mine.wait()


def total_over_tp(x, n, number):
    rows, columns = x.shape
    return pl.pallas_call(
        functools.partial(total_kernel, n),
        out_shape=jax.ShapeDtypeStruct(x.shape, x.dtype),
        in_specs=[pl.BlockSpec(memory_space=pltpu.VMEM)],
        out_specs=pl.BlockSpec(memory_space=pltpu.VMEM),
        scratch_shapes=[
            pltpu.VMEM((n - 1, rows, columns // n), x.dtype),
            pltpu.VMEM((rows, columns // n), x.dtype),
            pltpu.SemaphoreType.DMA(()),
            pltpu.SemaphoreType.DMA((2, n - 1)),
            pltpu.SemaphoreType.DMA((2, n - 1)),
        ],
        compiler_params=pltpu.CompilerParams(collective_id=number, has_side_effects=True),
    )(x)


def attend(queries, pool, table, lengths):
    row_count = queries.shape[0]
    slot_count = lengths.shape[0]
    page_size = pool.shape[2]
    kv_width = pool.shape[3] // HD
    group_size = queries.shape[1] // pool.shape[3]
    context = table.shape[1] * page_size
    prefill = row_count - slot_count + 1
    row_index = jnp.arange(row_count, dtype=jnp.int32)
    row_slot = jnp.maximum(row_index - prefill + 1, 0)
    slot_match = row_slot[:, None] == jnp.arange(slot_count, dtype=jnp.int32)[None, :]
    row_length = jnp.sum(jnp.where(slot_match, lengths[None, :], 0), axis=1)
    row_position = jnp.where(row_index < prefill, row_length - prefill + row_index, row_length - 1)
    pages = jnp.take(pool, table.reshape(-1), axis=0)
    keys = pages[:, 0].reshape(slot_count * context, kv_width, HD)
    values = pages[:, 1].reshape(slot_count * context, kv_width, HD)
    key_index = jnp.arange(slot_count * context, dtype=jnp.int32)
    valid = ((key_index // context)[None, :] == row_slot[:, None]) & (
        (key_index % context)[None, :] <= row_position[:, None]
    )
    shaped = queries.reshape(row_count, kv_width, group_size, HD)
    scores = jnp.einsum("rkgd,skd->rkgs", shaped, keys, preferred_element_type=jnp.float32) * (
        1.0 / HD**0.5
    )
    usable = valid[:, None, None, :]
    masked = jnp.where(usable, scores, -1e30)
    peak = jnp.max(masked, axis=3, keepdims=True)
    weights = jnp.where(usable, jnp.exp(masked - peak), 0.0)
    probs = (weights / jnp.sum(weights, axis=3, keepdims=True)).astype(jnp.bfloat16)
    mixed = jnp.einsum("rkgs,skd->rkgd", probs, values, preferred_element_type=jnp.float32)
    return mixed.reshape(row_count, kv_width * group_size * HD).astype(jnp.bfloat16)


def per_device(
    queries,
    kv_cache,
    page_table,
    cache_lengths,
    residual,
    out_weight,
    norm_gain,
    router,
    gate_weight,
    up_weight,
    down_weight,
    expert_ids,
):
    attended = attend(queries, kv_cache, page_table, cache_lengths)
    projected, laid = project(attended, out_weight, down_weight[0], TP, 1)
    hidden_state = residual.astype(jnp.float32) + projected
    inverse = lax.rsqrt(jnp.mean(hidden_state * hidden_state, axis=1, keepdims=True) + 1e-05)
    normed = (hidden_state * inverse * norm_gain[None, :]).astype(jnp.bfloat16)
    logits = jnp.dot(normed, router, preferred_element_type=jnp.float32)
    expert_range = jnp.arange(EXPERTS, dtype=jnp.int32)
    chosen = jnp.sum(
        jnp.where(expert_ids[:, :, None] == expert_range[None, None, :], logits[:, None, :], 0.0),
        axis=2,
    )
    first = jax.nn.sigmoid(chosen[:, 0] - chosen[:, 1])
    mixing = jnp.stack([first, 1.0 - first], axis=1).reshape(-1)
    flat = expert_ids.reshape(-1)
    onehot = (flat[:, None] == expert_range[None, :]).astype(jnp.int32)
    before = jnp.cumsum(onehot, axis=0) - onehot
    slot = jnp.sum(before * onehot, axis=1)
    local_experts = gate_weight.shape[0]
    owned = lax.axis_index("tp") * local_experts + jnp.arange(local_experts, dtype=jnp.int32)
    capacity_range = jnp.arange(CAP, dtype=jnp.int32)
    select = (flat[None, None, :] == owned[:, None, None]) & (
        slot[None, None, :] == capacity_range[None, :, None]
    )
    repeated = jnp.repeat(normed, 2, axis=0)
    dispatched = jnp.einsum(
        "ecr,rd->ecd", select.astype(jnp.bfloat16), repeated, preferred_element_type=jnp.float32
    ).astype(jnp.bfloat16)[0]
    pieces = run_expert(dispatched, gate_weight[0], up_weight[0], laid, 3)
    pieces = pieces.reshape(NZ, CAP, NY, -1)
    outputs = jnp.where(
        lax.axis_index("tp") % 2 == 0,
        jnp.transpose(pieces, (1, 2, 0, 3)),
        jnp.transpose(pieces, (1, 0, 2, 3)),
    ).reshape(local_experts, CAP, D)
    gathered = jnp.einsum("ecr,ecd->rd", select.astype(jnp.float32), outputs)
    weighted = gathered * mixing[:, None]
    local_mix = jnp.sum(weighted.reshape(residual.shape[0], 2, D), axis=1)
    expert_mix = total_over_tp(local_mix.astype(jnp.bfloat16), TP, 5).astype(jnp.float32)
    return (hidden_state + expert_mix).astype(jnp.bfloat16)


def solution(mesh):
    return jax.shard_map(
        per_device,
        mesh=mesh,
        in_specs=(
            P("req", "tp"),
            P("req", None, None, "tp"),
            P("req", None),
            P("req"),
            P("req", None),
            P("req", "tp"),
            P(),
            P(),
            P("tp", None, "req"),
            P("tp", None, "req"),
            P("tp", "req", None),
            P("req", None),
        ),
        out_specs=P("req", None),
        check_vma=False,
    )
```

```python
import functools

import jax
import jax.numpy as jnp
from jax import lax
from jax.experimental import pallas as pl
from jax.experimental.pallas import tpu as pltpu
from jax.sharding import PartitionSpec as P

D = 4096
HD = 128
EXPERTS = 8
CAP = 8
TP = 8

MESH = pl.DeviceIdType.MESH
NY = 8
NZ = 8


def place_of(me, swap):
    y, z = me // NZ, me % NZ
    return z + swap * (y - z), y + swap * (z - y)


def index_of(a, b, swap):
    return (b + swap * (a - b)) * NZ + a + swap * (b - a)


def lay_down(place, swap, first, down_ref, laid_ref, lay_send, lay_recv):
    a, b = place
    laid = []
    for far in range(first, first + NZ // 2):
        for step in range(1, NY):
            to = (b + step) % NY
            width = pl.ds(pl.multiple_of(index_of(far, to, swap) * 128, 128), 128)
            copy = pltpu.make_async_remote_copy(
                src_ref=down_ref.at[:, width],
                dst_ref=laid_ref.at[b, :, pl.ds((far - first) * 128, 128)],
                send_sem=lay_send.at[step - 1, far - first],
                recv_sem=lay_recv.at[step - 1, far - first],
                device_id={"req": index_of(a, to, swap)},
                device_id_type=MESH,
            )
            copy.start()
            laid.append(copy)
    for far in range(first, first + NZ // 2):
        width = pl.ds(pl.multiple_of(index_of(far, b, swap) * 128, 128), 128)
        laid_ref[b, :, pl.ds((far - first) * 128, 128)] = down_ref[:, width]
    return laid


def project_kernel(
    n, x_ref, w_ref, down_ref, out_ref, laid_ref,
    rows_all, w_all, partial, landing, parts, own,
    own_sem, row_send, row_recv, ring_send, ring_recv, back_send, back_recv,
    sum_send, sum_recv, lay_send, lay_recv,
):
    me = lax.axis_index("req")
    t = lax.axis_index("tp")
    swap = t % 2
    a, b = place_of(me, swap)
    y, z = me // NZ, me % NZ
    barrier = pltpu.get_barrier_semaphore()
    for step in range(1, NY):
        for peer in (
            {"req": y * NZ + (z + step) % NZ},
            {"req": ((y + step) % NY) * NZ + z},
            {"tp": (t + step) % n},
        ):
            pl.semaphore_signal(barrier, inc=1, device_id=peer, device_id_type=MESH)
    pl.semaphore_wait(barrier, 2 * (NY - 1) + n - 1)

    sign = 1 - 2 * swap
    ring = {}
    spread = []
    for step in range(4):
        for way in (1, -1):
            if way == -1 and step == 3:
                continue
            if step:
                ring[way, step - 1].wait_recv()
            region = w_all.at[(z - sign * way * step + 2 * NZ) % NZ]
            copy = pltpu.make_async_remote_copy(
                src_ref=region if step else w_ref,
                dst_ref=region,
                send_sem=ring_send.at[(1 - way) // 2, step],
                recv_sem=ring_recv.at[(1 - way) // 2, step],
                device_id={"req": y * NZ + (z + sign * way + NZ) % NZ},
                device_id_type=MESH,
            )
            copy.start()
            ring[way, step] = copy
        if step == 0:
            for far in range(1, NY):
                copy = pltpu.make_async_remote_copy(
                    src_ref=x_ref,
                    dst_ref=rows_all.at[y],
                    send_sem=row_send.at[far - 1],
                    recv_sem=row_recv.at[far - 1],
                    device_id={"req": ((y + far) % NY) * NZ + z},
                    device_id_type=MESH,
                )
                copy.start()
                spread.append(copy)
            rows_all[y] = x_ref[...]
            w_all[z] = w_ref[...]
    ring[1, 3].wait_recv()
    ring[-1, 2].wait_recv()
    for copy in spread:
        copy.wait_recv()
    depth = x_ref.shape[1]
    product = lax.dot_general(
        rows_all[...].reshape(-1, depth),
        w_all[...].reshape(-1, depth),
        (((1,), (1,)), ((), ())),
        preferred_element_type=jnp.float32,
    )
    partial[...] = product.astype(partial.dtype).reshape(partial.shape)
    back = []
    for far in range(1, NY):
        to = (y + far) % NY
        copy = pltpu.make_async_remote_copy(
            src_ref=partial.at[to],
            dst_ref=landing.at[y],
            send_sem=back_send.at[far - 1],
            recv_sem=back_recv.at[far - 1],
            device_id={"req": to * NZ + z},
            device_id_type=MESH,
        )
        copy.start()
        back.append(copy)
    landing[y] = partial[y]
    laid = lay_down((a, b), swap, 0, down_ref, laid_ref, lay_send, lay_recv)
    for copy in back:
        copy.wait_recv()

    def columns(index):
        return pl.ds(pl.multiple_of(index * landing.shape[2], landing.shape[2]), landing.shape[2])

    scatter = []
    for step in range(1, n):
        peer = (t + step) % n
        copy = pltpu.make_async_remote_copy(
            src_ref=landing.at[peer],
            dst_ref=parts.at[step - 1],
            send_sem=sum_send.at[0, step - 1],
            recv_sem=sum_recv.at[0, step - 1],
            device_id={"tp": peer},
            device_id_type=MESH,
        )
        copy.start()
        scatter.append(copy)
    total = landing[t].astype(jnp.float32)
    for step in range(1, n):
        scatter[step - 1].wait_recv()
        total = total + parts[step - 1].astype(jnp.float32)
    own[...] = total
    share = []
    for step in range(1, n):
        copy = pltpu.make_async_remote_copy(
            src_ref=own,
            dst_ref=out_ref.at[:, columns(t)],
            send_sem=sum_send.at[1, step - 1],
            recv_sem=sum_recv.at[1, step - 1],
            device_id={"tp": (t + step) % n},
            device_id_type=MESH,
        )
        copy.start()
        share.append(copy)
    mine = pltpu.make_async_copy(own, out_ref.at[:, columns(t)], own_sem)
    mine.start()
    for copy in share:
        copy.wait_recv()
    for copy in laid:
        copy.wait_recv()
    for copy in [*ring.values(), *spread, *back, *scatter, *share, *laid]:
        copy.wait_send()
    mine.wait()


def project(attended, weight, down, n, number):
    rows, depth = attended.shape
    outs = weight.shape[0]
    wide = NZ * outs
    vmem = pl.BlockSpec(memory_space=pltpu.VMEM)
    dma = pltpu.SemaphoreType.DMA
    return pl.pallas_call(
        functools.partial(project_kernel, n),
        out_shape=[
            jax.ShapeDtypeStruct((rows, NY * wide), jnp.float32),
            jax.ShapeDtypeStruct((NY, down.shape[0], down.shape[1] // NY // 2), down.dtype),
        ],
        in_specs=[vmem] * 3,
        out_specs=[vmem] * 2,
        scratch_shapes=[
            pltpu.VMEM((NY, rows, depth), attended.dtype),
            pltpu.VMEM((NZ, outs, depth), weight.dtype),
            pltpu.VMEM((NY, rows, wide), jnp.bfloat16),
            pltpu.VMEM((NY, rows, wide), jnp.bfloat16),
            pltpu.VMEM((n - 1, rows, wide), jnp.bfloat16),
            pltpu.VMEM((rows, wide), jnp.float32),
            dma(()),
            dma((7,)), dma((7,)),
            dma((2, 4)), dma((2, 4)),
            dma((7,)), dma((7,)),
            dma((2, n - 1)), dma((2, n - 1)),
            dma((7, 4)), dma((7, 4)),
        ],
        compiler_params=pltpu.CompilerParams(collective_id=number, has_side_effects=True),
    )(attended, weight, down)


def moe_kernel(
    x_ref, gate_ref, up_ref, laid_ref, down_ref, out_ref,
    held, both, products, units, partial, landing, late,
    own_sem, hop_send, hop_recv, ring_send, ring_recv, send_sem, recv_sem, lay_send, lay_recv,
):
    me = lax.axis_index("req")
    swap = lax.axis_index("tp") % 2
    sign = 1 - 2 * swap
    y, z = me // NZ, me % NZ
    a, b = place_of(me, swap)

    def at_z(step):
        return (z + sign * step + 2 * NZ) % NZ

    def at_y(step):
        return (y + sign * step + 2 * NY) % NY

    neighbours = [
        {1: y * NZ + at_z(1), -1: y * NZ + at_z(-1)},
        {1: at_y(1) * NZ + z, -1: at_y(-1) * NZ + z},
    ]
    groups = NY * NZ
    barrier = pltpu.get_barrier_semaphore()

    @pl.loop(1, groups)
    def _(step):
        pl.semaphore_signal(
            barrier, inc=1, device_id={"req": (me + step) % groups}, device_id_type=MESH
        )

    both[:, : gate_ref.shape[1]] = gate_ref[...]
    both[:, gate_ref.shape[1] :] = up_ref[...]
    products[...] = jnp.zeros_like(products)
    pl.semaphore_wait(barrier, groups - 1)
    own = pltpu.make_async_copy(x_ref, held.at[y, z], own_sem)
    own.start()
    columns = x_ref.shape[1]
    halves = [
        (slice(None), pl.ds(0, columns // 2)),
        (slice(None), pl.ds(columns // 2, columns // 2)),
    ]

    plan = []
    for half in range(2):
        for way, steps in ((1, 4), (-1, 3)):
            for step in range(steps):
                needs = (half, 1, way, 0, step - 1) if step else None
                plan.append((step, 0, (half, 1, way, 0, step), needs))
                for far in (0, -1, 1, -2, 2, -3, 3, -4):
                    if step:
                        needs = (half, 2, way, far, step - 1)
                    elif far:
                        needs = (half, 1, 1 if far < 0 else -1, 0, abs(far) - 1)
                    else:
                        needs = None
                    plan.append((abs(far) + step, 1, (half, 2, way, far, step), needs))
    plan.sort(key=lambda entry: entry[:2])
    hops, landed = {}, set()
    for entry, (_, _, key, needs) in enumerate(plan):
        half, phase, way, far, step = key
        if needs is not None and needs not in landed:
            hops[needs].wait_recv()
            landed.add(needs)
        one, two = (-way * step, 0) if phase == 1 else (far, -way * step)
        where = (at_y(two), at_z(one)) if half == 0 else (at_y(one), at_z(two))
        region = held.at[where + halves[half]]
        first = step == 0 and far == 0
        copy = pltpu.make_async_remote_copy(
            src_ref=x_ref.at[halves[half]] if first else region,
            dst_ref=region,
            send_sem=hop_send.at[entry],
            recv_sem=hop_recv.at[entry],
            device_id={"req": neighbours[(half + phase - 1) % 2][way]},
            device_id_type=MESH,
        )
        copy.start()
        hops[key] = copy
    laid = lay_down((a, b), swap, NZ // 2, down_ref, late, lay_send, lay_recv)
    for key, copy in hops.items():
        if key not in landed:
            copy.wait_recv()
    own.wait()
    depth = 512
    width = gate_ref.shape[1]

    @pl.loop(0, columns // depth)
    def _(step):
        span = pl.ds(pl.multiple_of(step * depth, depth), depth)
        block = held[:, :, :, span].reshape(products.shape[0], depth)
        products[...] += jnp.dot(block, both[span, :], preferred_element_type=jnp.float32)

    gate = products[:, :width]
    active = (gate / (1.0 + jnp.exp(-gate)) * products[:, width:]).astype(units.dtype)

    def block(step):
        return pl.ds(pl.multiple_of(((a + step + NZ) % NZ) * 128, 128), 128)

    units[:, block(0)] = active
    copies = {}
    depth = units.shape[0] // 2
    for step in range(4):
        for way in (1, -1):
            for part in range(2):
                if step == 3 and part != (1 - way) // 2:
                    continue
                if step:
                    copies[way, part, step - 1].wait_recv()
                region = units.at[pl.ds(part * depth, depth), block(-way * step)]
                copy = pltpu.make_async_remote_copy(
                    src_ref=region,
                    dst_ref=region,
                    send_sem=ring_send.at[(1 - way) // 2, part, step],
                    recv_sem=ring_recv.at[(1 - way) // 2, part, step],
                    device_id={"req": index_of((a + way + NZ) % NZ, b, swap)},
                    device_id_type=MESH,
                )
                copy.start()
                copies[way, part, step] = copy
    for key in ((1, 0, 3), (-1, 1, 3), (1, 1, 2), (-1, 0, 2)):
        copies[key].wait_recv()
    for copy in laid:
        copy.wait_recv()
    product = None
    for number, weights_ref in enumerate((laid_ref, late)):
        span = weights_ref.shape[2]
        term = lax.dot_general(
            units[:, number * span : (number + 1) * span],
            weights_ref[...].reshape(-1, span),
            (((1,), (1,)), ((), ())),
            preferred_element_type=jnp.float32,
        )
        product = term if product is None else product + term
    partial[...] = product.astype(partial.dtype).reshape(partial.shape)

    def message(step):
        to = (me + step) % groups
        return pltpu.make_async_remote_copy(
            src_ref=partial.at[to],
            dst_ref=landing.at[b * NZ + a],
            send_sem=send_sem.at[step - 1],
            recv_sem=recv_sem.at[step - 1],
            device_id={"req": to},
            device_id_type=MESH,
        )

    @pl.loop(1, groups)
    def _(step):
        message(step).start()

    landing[b * NZ + a] = partial[me]

    @pl.loop(1, groups)
    def _(step):
        message(step).wait_recv()

    total = landing[pl.ds(0, NZ)].astype(jnp.float32)
    for row in range(1, NY):
        total = total + landing[pl.ds(row * NZ, NZ)].astype(jnp.float32)
    out_ref[...] = total

    @pl.loop(1, groups)
    def _(step):
        message(step).wait_send()

    for copy in [*hops.values(), *copies.values(), *laid]:
        copy.wait_send()


def run_expert(rows, gate, up, laid, down, number):
    slots, columns = rows.shape
    width = gate.shape[1]
    outs = laid.shape[0] * laid.shape[1]
    groups = NY * NZ
    vmem = pl.BlockSpec(memory_space=pltpu.VMEM)
    dma = pltpu.SemaphoreType.DMA
    return pl.pallas_call(
        moe_kernel,
        out_shape=jax.ShapeDtypeStruct((NZ, slots, outs), jnp.float32),
        in_specs=[vmem] * 5,
        out_specs=vmem,
        scratch_shapes=[
            pltpu.VMEM((NY, NZ, slots, columns), rows.dtype),
            pltpu.VMEM((columns, 2 * width), gate.dtype),
            pltpu.VMEM((groups * slots, 2 * width), jnp.float32),
            pltpu.VMEM((groups * slots, NZ * width), rows.dtype),
            pltpu.VMEM((groups, slots, outs), jnp.bfloat16),
            pltpu.VMEM((groups, slots, outs), jnp.bfloat16),
            pltpu.VMEM(laid.shape, laid.dtype),
            dma(()),
            dma((126,)), dma((126,)),
            dma((2, 2, 4)), dma((2, 2, 4)),
            dma((groups - 1,)), dma((groups - 1,)),
            dma((7, 4)), dma((7, 4)),
        ],
        compiler_params=pltpu.CompilerParams(collective_id=number, has_side_effects=True),
    )(rows, gate, up, laid, down)


def total_kernel(n, x_ref, out_ref, parts, own, own_sem, send_sem, recv_sem):
    me = lax.axis_index("tp")
    width = x_ref.shape[1] // n
    barrier = pltpu.get_barrier_semaphore()
    for step in range(1, n):
        pl.semaphore_signal(
            barrier, inc=1, device_id={"tp": (me + step) % n}, device_id_type=MESH
        )
    pl.semaphore_wait(barrier, n - 1)

    def columns(index):
        return pl.ds(pl.multiple_of(index * width, width), width)

    scatter = []
    for step in range(1, n):
        peer = (me + step) % n
        copy = pltpu.make_async_remote_copy(
            src_ref=x_ref.at[:, columns(peer)],
            dst_ref=parts.at[step - 1],
            send_sem=send_sem.at[0, step - 1],
            recv_sem=recv_sem.at[0, step - 1],
            device_id={"tp": peer},
            device_id_type=MESH,
        )
        copy.start()
        scatter.append(copy)
    total = x_ref[:, columns(me)].astype(jnp.float32)
    for step in range(1, n):
        scatter[step - 1].wait_recv()
        total = total + parts[step - 1].astype(jnp.float32)
    own[...] = total.astype(own.dtype)
    spread = []
    for step in range(1, n):
        peer = (me + step) % n
        copy = pltpu.make_async_remote_copy(
            src_ref=own,
            dst_ref=out_ref.at[:, columns(me)],
            send_sem=send_sem.at[1, step - 1],
            recv_sem=recv_sem.at[1, step - 1],
            device_id={"tp": peer},
            device_id_type=MESH,
        )
        copy.start()
        spread.append(copy)
    mine = pltpu.make_async_copy(own, out_ref.at[:, columns(me)], own_sem)
    mine.start()
    for copy in scatter:
        copy.wait_send()
    for copy in spread:
        copy.wait_recv()
    for copy in spread:
        copy.wait_send()
    mine.wait()


def total_over_tp(x, n, number):
    rows, columns = x.shape
    return pl.pallas_call(
        functools.partial(total_kernel, n),
        out_shape=jax.ShapeDtypeStruct(x.shape, x.dtype),
        in_specs=[pl.BlockSpec(memory_space=pltpu.VMEM)],
        out_specs=pl.BlockSpec(memory_space=pltpu.VMEM),
        scratch_shapes=[
            pltpu.VMEM((n - 1, rows, columns // n), x.dtype),
            pltpu.VMEM((rows, columns // n), x.dtype),
            pltpu.SemaphoreType.DMA(()),
            pltpu.SemaphoreType.DMA((2, n - 1)),
            pltpu.SemaphoreType.DMA((2, n - 1)),
        ],
        compiler_params=pltpu.CompilerParams(collective_id=number, has_side_effects=True),
    )(x)


def attend(queries, pool, table, lengths):
    row_count = queries.shape[0]
    slot_count = lengths.shape[0]
    page_size = pool.shape[2]
    kv_width = pool.shape[3] // HD
    group_size = queries.shape[1] // pool.shape[3]
    context = table.shape[1] * page_size
    prefill = row_count - slot_count + 1
    row_index = jnp.arange(row_count, dtype=jnp.int32)
    row_slot = jnp.maximum(row_index - prefill + 1, 0)
    slot_match = row_slot[:, None] == jnp.arange(slot_count, dtype=jnp.int32)[None, :]
    row_length = jnp.sum(jnp.where(slot_match, lengths[None, :], 0), axis=1)
    row_position = jnp.where(row_index < prefill, row_length - prefill + row_index, row_length - 1)
    pages = jnp.take(pool, table.reshape(-1), axis=0)
    keys = pages[:, 0].reshape(slot_count * context, kv_width, HD)
    values = pages[:, 1].reshape(slot_count * context, kv_width, HD)
    key_index = jnp.arange(slot_count * context, dtype=jnp.int32)
    valid = ((key_index // context)[None, :] == row_slot[:, None]) & (
        (key_index % context)[None, :] <= row_position[:, None]
    )
    shaped = queries.reshape(row_count, kv_width, group_size, HD)
    scores = jnp.einsum("rkgd,skd->rkgs", shaped, keys, preferred_element_type=jnp.float32) * (
        1.0 / HD**0.5
    )
    usable = valid[:, None, None, :]
    masked = jnp.where(usable, scores, -1e30)
    peak = jnp.max(masked, axis=3, keepdims=True)
    weights = jnp.where(usable, jnp.exp(masked - peak), 0.0)
    probs = (weights / jnp.sum(weights, axis=3, keepdims=True)).astype(jnp.bfloat16)
    mixed = jnp.einsum("rkgs,skd->rkgd", probs, values, preferred_element_type=jnp.float32)
    return mixed.reshape(row_count, kv_width * group_size * HD).astype(jnp.bfloat16)


def per_device(
    queries,
    kv_cache,
    page_table,
    cache_lengths,
    residual,
    out_weight,
    norm_gain,
    router,
    gate_weight,
    up_weight,
    down_weight,
    expert_ids,
):
    attended = attend(queries, kv_cache, page_table, cache_lengths)
    projected, laid = project(attended, out_weight, down_weight[0], TP, 1)
    hidden_state = residual.astype(jnp.float32) + projected
    inverse = lax.rsqrt(jnp.mean(hidden_state * hidden_state, axis=1, keepdims=True) + 1e-05)
    normed = (hidden_state * inverse * norm_gain[None, :]).astype(jnp.bfloat16)
    logits = jnp.dot(normed, router, preferred_element_type=jnp.float32)
    expert_range = jnp.arange(EXPERTS, dtype=jnp.int32)
    chosen = jnp.sum(
        jnp.where(expert_ids[:, :, None] == expert_range[None, None, :], logits[:, None, :], 0.0),
        axis=2,
    )
    first = jax.nn.sigmoid(chosen[:, 0] - chosen[:, 1])
    mixing = jnp.stack([first, 1.0 - first], axis=1).reshape(-1)
    flat = expert_ids.reshape(-1)
    onehot = (flat[:, None] == expert_range[None, :]).astype(jnp.int32)
    before = jnp.cumsum(onehot, axis=0) - onehot
    slot = jnp.sum(before * onehot, axis=1)
    local_experts = gate_weight.shape[0]
    owned = lax.axis_index("tp") * local_experts + jnp.arange(local_experts, dtype=jnp.int32)
    capacity_range = jnp.arange(CAP, dtype=jnp.int32)
    select = (flat[None, None, :] == owned[:, None, None]) & (
        slot[None, None, :] == capacity_range[None, :, None]
    )
    repeated = jnp.repeat(normed, 2, axis=0)
    dispatched = jnp.einsum(
        "ecr,rd->ecd", select.astype(jnp.bfloat16), repeated, preferred_element_type=jnp.float32
    ).astype(jnp.bfloat16)[0]
    pieces = run_expert(dispatched, gate_weight[0], up_weight[0], laid, down_weight[0], 3)
    pieces = pieces.reshape(NZ, CAP, NY, -1)
    outputs = jnp.where(
        lax.axis_index("tp") % 2 == 0,
        jnp.transpose(pieces, (1, 2, 0, 3)),
        jnp.transpose(pieces, (1, 0, 2, 3)),
    ).reshape(local_experts, CAP, D)
    gathered = jnp.einsum("ecr,ecd->rd", select.astype(jnp.float32), outputs)
    weighted = gathered * mixing[:, None]
    local_mix = jnp.sum(weighted.reshape(residual.shape[0], 2, D), axis=1)
    expert_mix = total_over_tp(local_mix.astype(jnp.bfloat16), TP, 5).astype(jnp.float32)
    return (hidden_state + expert_mix).astype(jnp.bfloat16)


def solution(mesh):
    return jax.shard_map(
        per_device,
        mesh=mesh,
        in_specs=(
            P("req", "tp"),
            P("req", None, None, "tp"),
            P("req", None),
            P("req"),
            P("req", None),
            P("req", "tp"),
            P(),
            P(),
            P("tp", None, "req"),
            P("tp", None, "req"),
            P("tp", "req", None),
            P("req", None),
        ),
        out_specs=P("req", None),
        check_vma=False,
    )
```

```python
import functools

import jax
import jax.numpy as jnp
from jax import lax
from jax.experimental import pallas as pl
from jax.experimental.pallas import tpu as pltpu
from jax.sharding import PartitionSpec as P

D = 4096
HD = 128
EXPERTS = 8
CAP = 8
TP = 8

MESH = pl.DeviceIdType.MESH
NY = 8
NZ = 8


def place_of(me, swap):
    y, z = me // NZ, me % NZ
    return z + swap * (y - z), y + swap * (z - y)


def index_of(a, b, swap):
    return (b + swap * (a - b)) * NZ + a + swap * (b - a)


def lay_down(place, swap, first, down_ref, laid_ref, lay_send, lay_recv):
    a, b = place
    laid = []
    for far in range(first, first + NZ // 2):
        for step in range(1, NY):
            to = (b + step) % NY
            width = pl.ds(pl.multiple_of(index_of(far, to, swap) * 128, 128), 128)
            copy = pltpu.make_async_remote_copy(
                src_ref=down_ref.at[:, width],
                dst_ref=laid_ref.at[b, :, pl.ds((far - first) * 128, 128)],
                send_sem=lay_send.at[step - 1, far - first],
                recv_sem=lay_recv.at[step - 1, far - first],
                device_id={"req": index_of(a, to, swap)},
                device_id_type=MESH,
            )
            copy.start()
            laid.append(copy)
    for far in range(first, first + NZ // 2):
        width = pl.ds(pl.multiple_of(index_of(far, b, swap) * 128, 128), 128)
        laid_ref[b, :, pl.ds((far - first) * 128, 128)] = down_ref[:, width]
    return laid


def project_kernel(
    n, x_ref, w_ref, down_ref, out_ref, laid_ref,
    rows_all, w_all, partial, landing, parts, own,
    own_sem, row_send, row_recv, ring_send, ring_recv, back_send, back_recv,
    sum_send, sum_recv, lay_send, lay_recv,
):
    me = lax.axis_index("req")
    t = lax.axis_index("tp")
    swap = t % 2
    a, b = place_of(me, swap)
    y, z = me // NZ, me % NZ
    barrier = pltpu.get_barrier_semaphore()
    for step in range(1, NY):
        for peer in (
            {"req": y * NZ + (z + step) % NZ},
            {"req": ((y + step) % NY) * NZ + z},
            {"tp": (t + step) % n},
        ):
            pl.semaphore_signal(barrier, inc=1, device_id=peer, device_id_type=MESH)
    pl.semaphore_wait(barrier, 2 * (NY - 1) + n - 1)

    sign = 1 - 2 * swap
    ring = {}
    spread = []
    for step in range(4):
        for way in (1, -1):
            if way == -1 and step == 3:
                continue
            if step:
                ring[way, step - 1].wait_recv()
            region = w_all.at[(z - sign * way * step + 2 * NZ) % NZ]
            copy = pltpu.make_async_remote_copy(
                src_ref=region if step else w_ref,
                dst_ref=region,
                send_sem=ring_send.at[(1 - way) // 2, step],
                recv_sem=ring_recv.at[(1 - way) // 2, step],
                device_id={"req": y * NZ + (z + sign * way + NZ) % NZ},
                device_id_type=MESH,
            )
            copy.start()
            ring[way, step] = copy
        if step == 0:
            for far in range(1, NY):
                copy = pltpu.make_async_remote_copy(
                    src_ref=x_ref,
                    dst_ref=rows_all.at[y],
                    send_sem=row_send.at[far - 1],
                    recv_sem=row_recv.at[far - 1],
                    device_id={"req": ((y + far) % NY) * NZ + z},
                    device_id_type=MESH,
                )
                copy.start()
                spread.append(copy)
            rows_all[y] = x_ref[...]
            w_all[z] = w_ref[...]
    ring[1, 3].wait_recv()
    ring[-1, 2].wait_recv()
    for copy in spread:
        copy.wait_recv()
    depth = x_ref.shape[1]
    product = lax.dot_general(
        rows_all[...].reshape(-1, depth),
        w_all[...].reshape(-1, depth),
        (((1,), (1,)), ((), ())),
        preferred_element_type=jnp.float32,
    )
    partial[...] = product.astype(partial.dtype).reshape(partial.shape)
    back = []
    for far in range(1, NY):
        to = (y + far) % NY
        copy = pltpu.make_async_remote_copy(
            src_ref=partial.at[to],
            dst_ref=landing.at[y],
            send_sem=back_send.at[far - 1],
            recv_sem=back_recv.at[far - 1],
            device_id={"req": to * NZ + z},
            device_id_type=MESH,
        )
        copy.start()
        back.append(copy)
    landing[y] = partial[y]
    laid = lay_down((a, b), swap, 0, down_ref, laid_ref, lay_send, lay_recv)
    for copy in back:
        copy.wait_recv()

    def columns(index):
        return pl.ds(pl.multiple_of(index * landing.shape[2], landing.shape[2]), landing.shape[2])

    scatter = []
    for step in range(1, n):
        peer = (t + step) % n
        copy = pltpu.make_async_remote_copy(
            src_ref=landing.at[peer],
            dst_ref=parts.at[step - 1],
            send_sem=sum_send.at[0, step - 1],
            recv_sem=sum_recv.at[0, step - 1],
            device_id={"tp": peer},
            device_id_type=MESH,
        )
        copy.start()
        scatter.append(copy)
    total = landing[t].astype(jnp.float32)
    for step in range(1, n):
        scatter[step - 1].wait_recv()
        total = total + parts[step - 1].astype(jnp.float32)
    own[...] = total
    share = []
    for step in range(1, n):
        copy = pltpu.make_async_remote_copy(
            src_ref=own,
            dst_ref=out_ref.at[:, columns(t)],
            send_sem=sum_send.at[1, step - 1],
            recv_sem=sum_recv.at[1, step - 1],
            device_id={"tp": (t + step) % n},
            device_id_type=MESH,
        )
        copy.start()
        share.append(copy)
    mine = pltpu.make_async_copy(own, out_ref.at[:, columns(t)], own_sem)
    mine.start()
    for copy in share:
        copy.wait_recv()
    for copy in laid:
        copy.wait_recv()
    for copy in [*ring.values(), *spread, *back, *scatter, *share, *laid]:
        copy.wait_send()
    mine.wait()


def project(attended, weight, down, n, number):
    rows, depth = attended.shape
    outs = weight.shape[0]
    wide = NZ * outs
    vmem = pl.BlockSpec(memory_space=pltpu.VMEM)
    dma = pltpu.SemaphoreType.DMA
    return pl.pallas_call(
        functools.partial(project_kernel, n),
        out_shape=[
            jax.ShapeDtypeStruct((rows, NY * wide), jnp.float32),
            jax.ShapeDtypeStruct((NY, down.shape[0], down.shape[1] // NY // 2), down.dtype),
        ],
        in_specs=[vmem] * 3,
        out_specs=[vmem] * 2,
        scratch_shapes=[
            pltpu.VMEM((NY, rows, depth), attended.dtype),
            pltpu.VMEM((NZ, outs, depth), weight.dtype),
            pltpu.VMEM((NY, rows, wide), jnp.bfloat16),
            pltpu.VMEM((NY, rows, wide), jnp.bfloat16),
            pltpu.VMEM((n - 1, rows, wide), jnp.bfloat16),
            pltpu.VMEM((rows, wide), jnp.float32),
            dma(()),
            dma((7,)), dma((7,)),
            dma((2, 4)), dma((2, 4)),
            dma((7,)), dma((7,)),
            dma((2, n - 1)), dma((2, n - 1)),
            dma((7, 4)), dma((7, 4)),
        ],
        compiler_params=pltpu.CompilerParams(collective_id=number, has_side_effects=True),
    )(attended, weight, down)


def moe_kernel(
    x_ref, gate_ref, up_ref, laid_ref, down_ref, out_ref,
    held, both, products, units, partial, landing, late,
    own_sem, hop_send, hop_recv, ring_send, ring_recv, send_sem, recv_sem, lay_send, lay_recv,
):
    me = lax.axis_index("req")
    swap = lax.axis_index("tp") % 2
    sign = 1 - 2 * swap
    y, z = me // NZ, me % NZ
    a, b = place_of(me, swap)

    def at_z(step):
        return (z + sign * step + 2 * NZ) % NZ

    def at_y(step):
        return (y + sign * step + 2 * NY) % NY

    neighbours = [
        {1: y * NZ + at_z(1), -1: y * NZ + at_z(-1)},
        {1: at_y(1) * NZ + z, -1: at_y(-1) * NZ + z},
    ]
    groups = NY * NZ
    barrier = pltpu.get_barrier_semaphore()

    @pl.loop(1, groups)
    def _(step):
        pl.semaphore_signal(
            barrier, inc=1, device_id={"req": (me + step) % groups}, device_id_type=MESH
        )

    both[:, : gate_ref.shape[1]] = gate_ref[...]
    both[:, gate_ref.shape[1] :] = up_ref[...]
    products[...] = jnp.zeros_like(products)
    pl.semaphore_wait(barrier, groups - 1)
    own = pltpu.make_async_copy(x_ref, held.at[y, z], own_sem)
    own.start()
    columns = x_ref.shape[1]
    halves = [
        (slice(None), pl.ds(0, columns // 2)),
        (slice(None), pl.ds(columns // 2, columns // 2)),
    ]

    plan = []
    for half in range(2):
        for way, steps in ((1, 4), (-1, 3)):
            for step in range(steps):
                needs = (half, 1, way, 0, step - 1) if step else None
                plan.append((step, 0, (half, 1, way, 0, step), needs))
                for far in (0, -1, 1, -2, 2, -3, 3, -4):
                    if step:
                        needs = (half, 2, way, far, step - 1)
                    elif far:
                        needs = (half, 1, 1 if far < 0 else -1, 0, abs(far) - 1)
                    else:
                        needs = None
                    plan.append((abs(far) + step, 1, (half, 2, way, far, step), needs))
    plan.sort(key=lambda entry: entry[:2])
    hops, landed = {}, set()
    for entry, (_, _, key, needs) in enumerate(plan):
        half, phase, way, far, step = key
        if needs is not None and needs not in landed:
            hops[needs].wait_recv()
            landed.add(needs)
        one, two = (-way * step, 0) if phase == 1 else (far, -way * step)
        where = (at_y(two), at_z(one)) if half == 0 else (at_y(one), at_z(two))
        region = held.at[where + halves[half]]
        first = step == 0 and far == 0
        copy = pltpu.make_async_remote_copy(
            src_ref=x_ref.at[halves[half]] if first else region,
            dst_ref=region,
            send_sem=hop_send.at[entry],
            recv_sem=hop_recv.at[entry],
            device_id={"req": neighbours[(half + phase - 1) % 2][way]},
            device_id_type=MESH,
        )
        copy.start()
        hops[key] = copy
    laid = lay_down((a, b), swap, NZ // 2, down_ref, late, lay_send, lay_recv)
    for key, copy in hops.items():
        if key not in landed:
            copy.wait_recv()
    own.wait()
    width = gate_ref.shape[1]
    depth = units.shape[0] // 2

    def block(step):
        return pl.ds(pl.multiple_of(((a + step + NZ) % NZ) * 128, 128), 128)

    copies = {}

    def pass_on(way, part, step):
        region = units.at[pl.ds(part * depth, depth), block(-way * step)]
        copy = pltpu.make_async_remote_copy(
            src_ref=region,
            dst_ref=region,
            send_sem=ring_send.at[(1 - way) // 2, part, step],
            recv_sem=ring_recv.at[(1 - way) // 2, part, step],
            device_id={"req": index_of((a + way + NZ) % NZ, b, swap)},
            device_id_type=MESH,
        )
        copy.start()
        copies[way, part, step] = copy

    for part in range(2):
        rows = pl.ds(part * depth, depth)

        @pl.loop(0, columns // 512)
        def _(step):
            span = pl.ds(pl.multiple_of(step * 512, 512), 512)
            piece = held[pl.ds(part * NY // 2, NY // 2), :, :, span].reshape(depth, 512)
            products[rows, :] += jnp.dot(piece, both[span, :], preferred_element_type=jnp.float32)

        gate = products[rows, :width]
        active = gate / (1.0 + jnp.exp(-gate)) * products[rows, width:]
        units[rows, block(0)] = active.astype(units.dtype)
        for way in (1, -1):
            pass_on(way, part, 0)
    for step in range(1, 4):
        for part in range(2):
            for way in (1, -1):
                if step == 3 and part != (1 - way) // 2:
                    continue
                copies[way, part, step - 1].wait_recv()
                pass_on(way, part, step)
    for key in ((1, 0, 3), (-1, 1, 3), (1, 1, 2), (-1, 0, 2)):
        copies[key].wait_recv()
    for copy in laid:
        copy.wait_recv()
    product = None
    for number, weights_ref in enumerate((laid_ref, late)):
        span = weights_ref.shape[2]
        term = lax.dot_general(
            units[:, number * span : (number + 1) * span],
            weights_ref[...].reshape(-1, span),
            (((1,), (1,)), ((), ())),
            preferred_element_type=jnp.float32,
        )
        product = term if product is None else product + term
    partial[...] = product.astype(partial.dtype).reshape(partial.shape)

    def message(step):
        to = (me + step) % groups
        return pltpu.make_async_remote_copy(
            src_ref=partial.at[to],
            dst_ref=landing.at[b * NZ + a],
            send_sem=send_sem.at[step - 1],
            recv_sem=recv_sem.at[step - 1],
            device_id={"req": to},
            device_id_type=MESH,
        )

    @pl.loop(1, groups)
    def _(step):
        message(step).start()

    landing[b * NZ + a] = partial[me]

    @pl.loop(1, groups)
    def _(step):
        message(step).wait_recv()

    total = landing[pl.ds(0, NZ)].astype(jnp.float32)
    for row in range(1, NY):
        total = total + landing[pl.ds(row * NZ, NZ)].astype(jnp.float32)
    out_ref[...] = total

    @pl.loop(1, groups)
    def _(step):
        message(step).wait_send()

    for copy in [*hops.values(), *copies.values(), *laid]:
        copy.wait_send()


def run_expert(rows, gate, up, laid, down, number):
    slots, columns = rows.shape
    width = gate.shape[1]
    outs = laid.shape[0] * laid.shape[1]
    groups = NY * NZ
    vmem = pl.BlockSpec(memory_space=pltpu.VMEM)
    dma = pltpu.SemaphoreType.DMA
    return pl.pallas_call(
        moe_kernel,
        out_shape=jax.ShapeDtypeStruct((NZ, slots, outs), jnp.float32),
        in_specs=[vmem] * 5,
        out_specs=vmem,
        scratch_shapes=[
            pltpu.VMEM((NY, NZ, slots, columns), rows.dtype),
            pltpu.VMEM((columns, 2 * width), gate.dtype),
            pltpu.VMEM((groups * slots, 2 * width), jnp.float32),
            pltpu.VMEM((groups * slots, NZ * width), rows.dtype),
            pltpu.VMEM((groups, slots, outs), jnp.bfloat16),
            pltpu.VMEM((groups, slots, outs), jnp.bfloat16),
            pltpu.VMEM(laid.shape, laid.dtype),
            dma(()),
            dma((126,)), dma((126,)),
            dma((2, 2, 4)), dma((2, 2, 4)),
            dma((groups - 1,)), dma((groups - 1,)),
            dma((7, 4)), dma((7, 4)),
        ],
        compiler_params=pltpu.CompilerParams(collective_id=number, has_side_effects=True),
    )(rows, gate, up, laid, down)


def total_kernel(n, x_ref, out_ref, parts, own, own_sem, send_sem, recv_sem):
    me = lax.axis_index("tp")
    width = x_ref.shape[1] // n
    barrier = pltpu.get_barrier_semaphore()
    for step in range(1, n):
        pl.semaphore_signal(
            barrier, inc=1, device_id={"tp": (me + step) % n}, device_id_type=MESH
        )
    pl.semaphore_wait(barrier, n - 1)

    def columns(index):
        return pl.ds(pl.multiple_of(index * width, width), width)

    scatter = []
    for step in range(1, n):
        peer = (me + step) % n
        copy = pltpu.make_async_remote_copy(
            src_ref=x_ref.at[:, columns(peer)],
            dst_ref=parts.at[step - 1],
            send_sem=send_sem.at[0, step - 1],
            recv_sem=recv_sem.at[0, step - 1],
            device_id={"tp": peer},
            device_id_type=MESH,
        )
        copy.start()
        scatter.append(copy)
    total = x_ref[:, columns(me)].astype(jnp.float32)
    for step in range(1, n):
        scatter[step - 1].wait_recv()
        total = total + parts[step - 1].astype(jnp.float32)
    own[...] = total.astype(own.dtype)
    spread = []
    for step in range(1, n):
        peer = (me + step) % n
        copy = pltpu.make_async_remote_copy(
            src_ref=own,
            dst_ref=out_ref.at[:, columns(me)],
            send_sem=send_sem.at[1, step - 1],
            recv_sem=recv_sem.at[1, step - 1],
            device_id={"tp": peer},
            device_id_type=MESH,
        )
        copy.start()
        spread.append(copy)
    mine = pltpu.make_async_copy(own, out_ref.at[:, columns(me)], own_sem)
    mine.start()
    for copy in scatter:
        copy.wait_send()
    for copy in spread:
        copy.wait_recv()
    for copy in spread:
        copy.wait_send()
    mine.wait()


def total_over_tp(x, n, number):
    rows, columns = x.shape
    return pl.pallas_call(
        functools.partial(total_kernel, n),
        out_shape=jax.ShapeDtypeStruct(x.shape, x.dtype),
        in_specs=[pl.BlockSpec(memory_space=pltpu.VMEM)],
        out_specs=pl.BlockSpec(memory_space=pltpu.VMEM),
        scratch_shapes=[
            pltpu.VMEM((n - 1, rows, columns // n), x.dtype),
            pltpu.VMEM((rows, columns // n), x.dtype),
            pltpu.SemaphoreType.DMA(()),
            pltpu.SemaphoreType.DMA((2, n - 1)),
            pltpu.SemaphoreType.DMA((2, n - 1)),
        ],
        compiler_params=pltpu.CompilerParams(collective_id=number, has_side_effects=True),
    )(x)


def attend(queries, pool, table, lengths):
    row_count = queries.shape[0]
    slot_count = lengths.shape[0]
    page_size = pool.shape[2]
    kv_width = pool.shape[3] // HD
    group_size = queries.shape[1] // pool.shape[3]
    context = table.shape[1] * page_size
    prefill = row_count - slot_count + 1
    row_index = jnp.arange(row_count, dtype=jnp.int32)
    row_slot = jnp.maximum(row_index - prefill + 1, 0)
    slot_match = row_slot[:, None] == jnp.arange(slot_count, dtype=jnp.int32)[None, :]
    row_length = jnp.sum(jnp.where(slot_match, lengths[None, :], 0), axis=1)
    row_position = jnp.where(row_index < prefill, row_length - prefill + row_index, row_length - 1)
    pages = jnp.take(pool, table.reshape(-1), axis=0)
    keys = pages[:, 0].reshape(slot_count * context, kv_width, HD)
    values = pages[:, 1].reshape(slot_count * context, kv_width, HD)
    key_index = jnp.arange(slot_count * context, dtype=jnp.int32)
    valid = ((key_index // context)[None, :] == row_slot[:, None]) & (
        (key_index % context)[None, :] <= row_position[:, None]
    )
    shaped = queries.reshape(row_count, kv_width, group_size, HD)
    scores = jnp.einsum("rkgd,skd->rkgs", shaped, keys, preferred_element_type=jnp.float32) * (
        1.0 / HD**0.5
    )
    usable = valid[:, None, None, :]
    masked = jnp.where(usable, scores, -1e30)
    peak = jnp.max(masked, axis=3, keepdims=True)
    weights = jnp.where(usable, jnp.exp(masked - peak), 0.0)
    probs = (weights / jnp.sum(weights, axis=3, keepdims=True)).astype(jnp.bfloat16)
    mixed = jnp.einsum("rkgs,skd->rkgd", probs, values, preferred_element_type=jnp.float32)
    return mixed.reshape(row_count, kv_width * group_size * HD).astype(jnp.bfloat16)


def per_device(
    queries,
    kv_cache,
    page_table,
    cache_lengths,
    residual,
    out_weight,
    norm_gain,
    router,
    gate_weight,
    up_weight,
    down_weight,
    expert_ids,
):
    attended = attend(queries, kv_cache, page_table, cache_lengths)
    projected, laid = project(attended, out_weight, down_weight[0], TP, 1)
    hidden_state = residual.astype(jnp.float32) + projected
    inverse = lax.rsqrt(jnp.mean(hidden_state * hidden_state, axis=1, keepdims=True) + 1e-05)
    normed = (hidden_state * inverse * norm_gain[None, :]).astype(jnp.bfloat16)
    logits = jnp.dot(normed, router, preferred_element_type=jnp.float32)
    expert_range = jnp.arange(EXPERTS, dtype=jnp.int32)
    chosen = jnp.sum(
        jnp.where(expert_ids[:, :, None] == expert_range[None, None, :], logits[:, None, :], 0.0),
        axis=2,
    )
    first = jax.nn.sigmoid(chosen[:, 0] - chosen[:, 1])
    mixing = jnp.stack([first, 1.0 - first], axis=1).reshape(-1)
    flat = expert_ids.reshape(-1)
    onehot = (flat[:, None] == expert_range[None, :]).astype(jnp.int32)
    before = jnp.cumsum(onehot, axis=0) - onehot
    slot = jnp.sum(before * onehot, axis=1)
    local_experts = gate_weight.shape[0]
    owned = lax.axis_index("tp") * local_experts + jnp.arange(local_experts, dtype=jnp.int32)
    capacity_range = jnp.arange(CAP, dtype=jnp.int32)
    select = (flat[None, None, :] == owned[:, None, None]) & (
        slot[None, None, :] == capacity_range[None, :, None]
    )
    repeated = jnp.repeat(normed, 2, axis=0)
    dispatched = jnp.einsum(
        "ecr,rd->ecd", select.astype(jnp.bfloat16), repeated, preferred_element_type=jnp.float32
    ).astype(jnp.bfloat16)[0]
    pieces = run_expert(dispatched, gate_weight[0], up_weight[0], laid, down_weight[0], 3)
    pieces = pieces.reshape(NZ, CAP, NY, -1)
    outputs = jnp.where(
        lax.axis_index("tp") % 2 == 0,
        jnp.transpose(pieces, (1, 2, 0, 3)),
        jnp.transpose(pieces, (1, 0, 2, 3)),
    ).reshape(local_experts, CAP, D)
    gathered = jnp.einsum("ecr,ecd->rd", select.astype(jnp.float32), outputs)
    weighted = gathered * mixing[:, None]
    local_mix = jnp.sum(weighted.reshape(residual.shape[0], 2, D), axis=1)
    expert_mix = total_over_tp(local_mix.astype(jnp.bfloat16), TP, 5).astype(jnp.float32)
    return (hidden_state + expert_mix).astype(jnp.bfloat16)


def solution(mesh):
    return jax.shard_map(
        per_device,
        mesh=mesh,
        in_specs=(
            P("req", "tp"),
            P("req", None, None, "tp"),
            P("req", None),
            P("req"),
            P("req", None),
            P("req", "tp"),
            P(),
            P(),
            P("tp", None, "req"),
            P("tp", None, "req"),
            P("tp", "req", None),
            P("req", None),
        ),
        out_specs=P("req", None),
        check_vma=False,
    )
```
